256 devices in a mesh: seq: 64 (over y, z_hi, x, core), dp: 4 (over z_lo).
Axes of the slice: x: 4, y: 4, z: 8 (z_hi: 2, z_lo: 4; z = z_hi * 4 + z_lo), core: 2. Of those that a mesh axis runs over, the one named last changes fastest.
Arguments:
- inputs: bfloat16 [4, 64, 512, 512], P('dp', 'seq'), may hold values from -16 to 16
- norm_gain: float32 [512], replicated, may hold values from 0.25 to 1.75
- qkv_weight: bfloat16 [512, 1536], replicated, may hold values from -2 to 2
- out_weight: bfloat16 [512, 512], replicated, may hold values from -0.25 to 0.25
- out_cotan: bfloat16 [4, 64, 512, 512], P('dp', 'seq'), may hold values from -6 to 6
Outputs:
- input_grad: bfloat16 [4, 64, 512, 512], P('dp', 'seq')
- qkv_weight_grad: float32 [512, 1536], P('seq')
- out_weight_grad: float32 [512, 512], P('seq')
- gain_grad: float32 [512], P('seq')
The draws below stay inside these ranges and needn't reach their ends.
All inputs are finite; a program needn't handle non-finite values.
Results may differ from the reference program's by a relative error of at most 0.0091.
Values may be sent and summed in bfloat16 or wider, within the bound.
A program may use at most 64 MiB of HBM per device.

```python
import math
import jax
import jax.numpy as jnp
from jax import lax

D = 512
H = 8
HD = 64
COLS = 512
NROWS = 64
BATCH = 4


def draw_qkv_weight(key, part):
    sampled = jax.random.normal(key, (D, 3 * D), jnp.float32) * D ** (-0.5)
    return jnp.clip(sampled, -2.0, 2.0).astype(jnp.bfloat16)


def strengthened(values, stream_key, source, target, shards_of, factor):
    def block_of(axis_at):
        return (jnp.arange(values.shape[axis_at]) // (values.shape[axis_at] // shards_of)).reshape((-1,) + (1,) * (values.ndim - 1 - axis_at))

    near = jax.random.permutation(stream_key, shards_of)[block_of(target)]
    other_side = (block_of(target) + shards_of // 2) % shards_of
    return jnp.where((block_of(source) == near) | (block_of(source) == other_side), factor * values, values)


def steps_of(own_key, dims, split, least, largest):
    def one(dim, blocks):
        heights = jax.random.uniform(jax.random.fold_in(jax.random.fold_in(own_key, 6), dim), (blocks,), jnp.float32, least / len(split), largest / len(split))
        return jnp.repeat(jnp.exp(heights), dims[dim] // blocks).reshape((-1,) + (1,) * (len(dims) - dim - 1))

    factor_of = one(*split[0])
    for cut in split[1:]:
        factor_of = factor_of * one(*cut)
    return factor_of


def gaussian(rng, shape, scale, limit, cuts=(), kind=jnp.bfloat16):
    entries = jax.random.normal(rng, shape, jnp.float32) * scale
    if len(cuts) > 0:
        entries = steps_of(rng, shape, cuts, -0.22, 0.18) * entries
    return jnp.clip(entries, min=-limit, max=limit).astype(kind)


def gaussian_with(key, dims, scale, reach, shards, heavy, kind=jnp.bfloat16):
    values = scale * jax.random.normal(key, dims, jnp.float32)
    if shards:
        values = values * steps_of(key, dims, shards, -0.22, 0.18)
    return jnp.clip(strengthened(values, jax.random.fold_in(key, 3), *heavy), -reach, reach).astype(kind)


def setup_inputs(seed: int = 0) -> dict:
    key_of = jax.random.split(jax.random.key(seed), 6)
    inputs = gaussian_with(key_of[0], (BATCH, NROWS, COLS, D), 1.0, 16.0, ((0, 4), (1, 64)), (1, 3, 64, 4.0))
    norm_gain = jnp.clip(1.0 + 0.15 * jax.random.normal(key_of[1], (D,), jnp.float32), 0.25, 1.75)
    qkv_weight = draw_qkv_weight(jax.random.fold_in(key_of[5], 71), 0)
    out_weight = gaussian(key_of[3], (D, D), D ** -0.5, 0.25)
    out_cotan = gaussian(key_of[4], (BATCH, NROWS, COLS, D), 1.0, 6.0, ((0, 4), (1, 64)))
    return {"inputs": inputs, "norm_gain": norm_gain, "qkv_weight": qkv_weight, "out_weight": out_weight, "out_cotan": out_cotan}


def blocked(kernel, arrays, group_size):
    block_count = arrays[0].shape[0] // group_size
    split_arrays = tuple((member.reshape((block_count, group_size) + member.shape[1:]) for member in arrays))
    result = lax.map(lambda pieces: kernel(*pieces), split_arrays)
    return jax.tree.map(lambda member: member.reshape((block_count * group_size,) + member.shape[2:]), result)

def attend_probs(queries, key_vals):
    score_scale = HD ** (-0.5)
    scores = jnp.einsum('glhd,gmhd->ghlm', queries.astype(jnp.float32), key_vals.astype(jnp.float32)) * score_scale
    length = queries.shape[1]
    causal = lax.broadcasted_iota(jnp.int32, (length, length), 0) >= lax.broadcasted_iota(jnp.int32, (length, length), 1)
    scores = jnp.where(causal, scores, -1e+30)
    row_max = lax.optimization_barrier(jnp.max(scores, -1, keepdims=True))
    exponent = jnp.exp(scores - row_max)
    return exponent / lax.optimization_barrier(jnp.sum(exponent, -1, keepdims=True))

def forward_block(queries, key_vals, values):
    weights = attend_probs(queries, key_vals).astype(jnp.bfloat16)
    return jnp.einsum('ghlm,gmhd->glhd', weights.astype(jnp.float32), values.astype(jnp.float32)).astype(jnp.bfloat16)

def backward_block(queries, key_vals, values, attended, cotangent):
    score_scale = HD ** (-0.5)
    softmax_probs = attend_probs(queries, key_vals)
    weights = softmax_probs.astype(jnp.bfloat16)
    cot_float = cotangent.astype(jnp.float32)
    prob_grad = jnp.einsum('glhd,gmhd->ghlm', cot_float, values.astype(jnp.float32))
    row_delta = lax.optimization_barrier(jnp.sum(cot_float * attended.astype(jnp.float32), -1))
    row_delta = jnp.transpose(row_delta, (0, 2, 1))[..., None]
    score_grad = (softmax_probs * (prob_grad - row_delta)).astype(jnp.bfloat16).astype(jnp.float32)
    grad_query = (jnp.einsum('ghlm,gmhd->glhd', score_grad, key_vals.astype(jnp.float32)) * score_scale).astype(jnp.bfloat16)
    grad_keys = (jnp.einsum('ghlm,glhd->gmhd', score_grad, queries.astype(jnp.float32)) * score_scale).astype(jnp.bfloat16)
    grad_values = jnp.einsum('ghlm,glhd->gmhd', weights.astype(jnp.float32), cot_float).astype(jnp.bfloat16)
    return (grad_query, grad_keys, grad_values)

def one_sequence(seq_input, norm_gain, qkv_weight, out_weight, seq_cotan):
    half_heads = H // 2
    tokens = NROWS * COLS
    flat_input = seq_input.reshape(tokens, D).astype(jnp.float32)
    inverse_rms = lax.rsqrt(lax.optimization_barrier(jnp.mean(flat_input * flat_input, -1, keepdims=True)) + 1e-05)
    normed = flat_input * inverse_rms
    hidden = (normed * norm_gain).astype(jnp.bfloat16)
    projected = jnp.dot(hidden, qkv_weight, preferred_element_type=jnp.float32).astype(jnp.bfloat16)
    flat_cotan = seq_cotan.reshape(tokens, D)
    grad_att = jnp.dot(flat_cotan, out_weight.T, preferred_element_type=jnp.float32).astype(jnp.bfloat16)
    qkv_grid = projected.reshape(NROWS, COLS, 3, H, HD)
    att_cot_grid = grad_att.reshape(NROWS, COLS, H, HD)
    row_group = math.gcd(NROWS, max(1, 512 // COLS))
    rows_in = (qkv_grid[:, :, 0, :half_heads], qkv_grid[:, :, 1, :half_heads], qkv_grid[:, :, 2, :half_heads])
    row_att = blocked(forward_block, rows_in, row_group)
    row_grads = blocked(backward_block, rows_in + (row_att, att_cot_grid[:, :, :half_heads]), row_group)
    col_grid = jnp.swapaxes(qkv_grid[:, :, :, half_heads:], 0, 1)
    col_cot = jnp.swapaxes(att_cot_grid[:, :, half_heads:], 0, 1)
    col_group = math.gcd(COLS, max(1, 512 // NROWS))
    cols_in = (col_grid[:, :, 0], col_grid[:, :, 1], col_grid[:, :, 2])
    col_att = blocked(forward_block, cols_in, col_group)
    col_grads = blocked(backward_block, cols_in + (col_att, col_cot), col_group)
    attended = jnp.concatenate([row_att, jnp.swapaxes(col_att, 0, 1)], 2).reshape(tokens, D)
    row_dqkv = jnp.stack(row_grads, 2)
    col_dqkv = jnp.swapaxes(jnp.stack(col_grads, 2), 0, 1)
    grad_qkv = jnp.concatenate([row_dqkv, col_dqkv], 3).reshape(tokens, 3 * D)
    term_out = jnp.dot(attended.T, flat_cotan, preferred_element_type=jnp.float32)
    term_qkv = jnp.dot(hidden.T, grad_qkv, preferred_element_type=jnp.float32)
    grad_hidden = jnp.dot(grad_qkv, qkv_weight.T, preferred_element_type=jnp.float32)
    term_gain = lax.optimization_barrier(jnp.sum(grad_hidden * normed, 0))
    grad_normed = grad_hidden * norm_gain
    grad_input = inverse_rms * (grad_normed - normed * lax.optimization_barrier(jnp.mean(grad_normed * normed, -1, keepdims=True)))
    seq_grad = (flat_cotan.astype(jnp.float32) + grad_input).astype(jnp.bfloat16).reshape(NROWS, COLS, D)
    return (seq_grad, term_qkv, term_out, term_gain)

def reference(inputs, norm_gain, qkv_weight, out_weight, out_cotan):
    outputs = []
    total_qkv = jnp.zeros((D, 3 * D), jnp.float32)
    total_out = jnp.zeros((D, D), jnp.float32)
    total_gain = jnp.zeros((D,), jnp.float32)
    for seq_index in range(BATCH):
        seq_grad, term_qkv, term_out, term_gain = one_sequence(inputs[seq_index], norm_gain, qkv_weight, out_weight, out_cotan[seq_index])
        outputs.append(seq_grad)
        total_qkv = total_qkv + term_qkv
        total_out = total_out + term_out
        total_gain = total_gain + term_gain
    return (jnp.stack(outputs, 0), total_qkv, total_out, total_gain)
```

```python
import jax
import jax.numpy as jnp
from jax import lax
from jax.experimental import pallas as pl
from jax.experimental.pallas import tpu as pltpu
from jax.sharding import PartitionSpec as P

MESH = pl.DeviceIdType.MESH
BF = jnp.bfloat16
F32 = jnp.float32
TOK = 512
D = 512
HALF = 256
HD = 64
RANKS = 64
LINE = 4
NC = 2048 + 128
CH = 128


def dot(a, b, ca, cb):
    return lax.dot_general(a, b, (((ca,), (cb,)), ((), ())), preferred_element_type=F32)


def rows8(ref, i):
    return ref[pl.ds(i * (CH // 8), CH // 8)].astype(F32).reshape(CH, D)


def norm_of(x):
    inv = lax.rsqrt(jnp.mean(x * x, -1, keepdims=True) + 1e-05)
    return inv, x * inv


def prepare(x_ref, c_ref, g_ref, hid_t, cot):
    def step(i, carry):
        x = rows8(x_ref, i)
        _, normed = norm_of(x)
        at = pl.multiple_of(i * CH, CH)
        hid_t[:, pl.ds(at, CH)] = (normed * g_ref[...]).T.astype(BF)
        cot[pl.ds(at, CH), :] = rows8(c_ref, i).astype(BF)
        return carry

    lax.fori_loop(0, TOK // CH, step, 0)


def project(w_ref, wo_ref, off, hid_t, cot, qkv_t, ga_t):
    for part in range(3):
        p = dot(w_ref[:, part * D + off : part * D + off + HALF], hid_t[...], 0, 0).astype(BF)
        if part == 0:
            p = p * BF(HD**-0.5)
        qkv_t[part * HALF : (part + 1) * HALF, :] = p
    ga_t[...] = dot(wo_ref[off : off + HALF, :], cot[...], 1, 1).astype(BF)


def attend(is_col, qkv_t, ga_t, att_t, d_t):
    qb = TOK // 2

    def head(h, carry):
        at = pl.multiple_of(h * HD, HD)
        sl = pl.ds(at, HD)
        dk = dv = None
        for b in range(2):
            kl = qb * (b + 1)
            qs = slice(b * qb, (b + 1) * qb)
            q = qkv_t[sl, qs]
            k = qkv_t[pl.ds(HALF + at, HD), :kl]
            v = qkv_t[pl.ds(2 * HALF + at, HD), :kl]
            ga = ga_t[sl, qs]
            s = dot(k, q, 0, 0)
            gap = (
                lax.broadcasted_iota(jnp.int32, (kl, qb), 1)
                + b * qb
                - lax.broadcasted_iota(jnp.int32, (kl, qb), 0)
            )
            allowed = gap >= 0
            if is_col:
                allowed = jnp.logical_and(allowed, jnp.bitwise_and(gap, 7) == 0)
            s = jnp.where(allowed, s, -1e30)
            e = jnp.exp(s - jnp.max(s, 0, keepdims=True))
            p = e * (1.0 / jnp.sum(e, 0, keepdims=True))
            w = p.astype(BF)
            o = dot(v, w, 1, 0).astype(BF)
            att_t[sl, qs] = o
            dp = dot(v, ga, 0, 0)
            delta = jnp.sum(ga.astype(F32) * o.astype(F32), 0, keepdims=True)
            ds = (p * (dp - delta)).astype(BF)
            d_t[sl, qs] = (dot(k, ds, 1, 0) * (HD**-0.5)).astype(BF)
            dkb, dvb = dot(q, ds, 1, 1), dot(ga, w, 1, 1)
            if b == 0:
                dk, dv = dkb, dvb
            else:
                dk = jnp.concatenate([dk + dkb[:, :qb], dkb[:, qb:]], 1)
                dv = jnp.concatenate([dv + dvb[:, :qb], dvb[:, qb:]], 1)
        d_t[pl.ds(HALF + at, HD), :] = dk.astype(BF)
        d_t[pl.ds(2 * HALF + at, HD), :] = dv.astype(BF)
        return carry

    lax.fori_loop(0, HALF // HD, head, 0)


def hidden_grad(w_ref, off, d_t, dh):
    for part in range(3):
        d = d_t[part * HALF : (part + 1) * HALF, :]
        term = dot(d, w_ref[:, part * D + off : part * D + off + HALF], 0, 1)
        if part == 0:
            dh[...] = term
        else:
            dh[...] += term


def weight_grads(off, base, hid_t, cot, att_t, d_t, terms):
    for part in range(3):
        d = d_t[part * HALF : (part + 1) * HALF, :]
        at = base + part * HALF
        terms[:, :, at : at + HALF] = dot(hid_t[...], d, 1, 1).reshape(RANKS, 8, HALF)
    half = slice(off // 8, (off + HALF) // 8)
    terms[half, :, 3 * D : 4 * D] = dot(att_t[...], cot[...], 1, 0).reshape(HALF // 8, 8, D)


def gain_term(x_ref, dh):
    def step(i, total):
        _, normed = norm_of(rows8(x_ref, i))
        at = pl.multiple_of(i * CH, CH)
        return total + jnp.sum(dh[pl.ds(at, CH), :] * normed, 0, keepdims=True)

    return lax.fori_loop(0, TOK // CH, step, jnp.zeros((1, D), F32))


def kernel(
    x_ref, c_ref, g_ref, w_ref, wo_ref,
    out_ref, gq_ref, go_ref, gg_ref,
    xr, cr, hid_t, cot, qkv_t, ga_t, att_t, d_t, dh_row, dh_col, dh_send, dh_recv,
    terms, core_send, core_recv, plane_send, plane_recv, z_sum, z_send, z_recv,
    send_sem, recv_sem, own_sem,
):
    me = lax.axis_index("seq")
    line = lax.axis_index("dp")
    core = me % 2
    z_hi = (me // 8) % 2
    plane = (me // 16) * 4 + (me // 2) % 4

    def rank_of(other, hi):
        return (other // 4) * 16 + hi * 8 + (other % 4) * 2 + core

    def remote(src, dst, i, target):
        return pltpu.make_async_remote_copy(
            src, dst, send_sem.at[i], recv_sem.at[i], device_id=target, device_id_type=MESH
        )

    def peer(t):
        return lax.rem(me + t, RANKS)

    def each_peer(f):
        def step(t, carry):
            f(peer(t))
            return carry

        lax.fori_loop(1, RANKS, step, 0)

    def each_line_peer(f):
        def step(t, carry):
            z = lax.rem(z_hi * LINE + line + t, 2 * LINE)
            f(z // LINE, z % LINE)
            return carry

        lax.fori_loop(1, 2 * LINE, step, 0)

    barrier = pltpu.get_barrier_semaphore()
    each_peer(lambda t: pl.semaphore_signal(barrier, inc=1, device_id={"seq": t}, device_id_type=MESH))
    for hi in range(2):
        for t in range(1, LINE):
            pl.semaphore_signal(
                barrier,
                inc=1,
                device_id={"seq": rank_of(plane, hi), "dp": lax.rem(line + t, LINE)},
                device_id_type=MESH,
            )
    pl.semaphore_wait(barrier, RANKS - 1 + 2 * (LINE - 1))

    def send_in(t):
        remote(x_ref.at[t], xr.at[me], 0, {"seq": t}).start()
        remote(c_ref.at[t], cr.at[me], 1, {"seq": t}).start()

    each_peer(send_in)
    own_x = pltpu.make_async_copy(x_ref.at[me], xr.at[me], own_sem.at[0])
    own_c = pltpu.make_async_copy(c_ref.at[me], cr.at[me], own_sem.at[1])
    own_x.start()
    own_c.start()

    prepare(x_ref, c_ref, g_ref, hid_t, cot)
    project(w_ref, wo_ref, 0, hid_t, cot, qkv_t, ga_t)
    attend(False, qkv_t, ga_t, att_t, d_t)
    hidden_grad(w_ref, 0, d_t, dh_row)
    weight_grads(0, 0, hid_t, cot, att_t, d_t, terms)
    gain_row = gain_term(x_ref, dh_row)

    own_x.wait()
    own_c.wait()
    rest = pl.ds(0, RANKS - 1)
    in_x = remote(x_ref.at[rest], xr.at[rest], 0, {"seq": me})
    in_c = remote(c_ref.at[rest], cr.at[rest], 1, {"seq": me})
    in_x.wait_recv()
    in_c.wait_recv()

    prepare(xr, cr, g_ref, hid_t, cot)
    project(w_ref, wo_ref, HALF, hid_t, cot, qkv_t, ga_t)
    attend(True, qkv_t, ga_t, att_t, d_t)
    hidden_grad(w_ref, HALF, d_t, dh_col)

    def round_out(i, carry):
        at = pl.multiple_of(i * CH, CH)
        dh_send[pl.ds(i * (CH // 8), CH // 8)] = dh_col[pl.ds(at, CH), :].reshape(CH // 8, 8, D).astype(BF)
        return carry

    lax.fori_loop(0, TOK // CH, round_out, 0)
    each_peer(lambda t: remote(dh_send.at[t], dh_recv.at[me], 2, {"seq": t}).start())
    own_h = pltpu.make_async_copy(dh_send.at[me], dh_recv.at[me], own_sem.at[0])
    own_h.start()

    weight_grads(HALF, 3 * HALF, hid_t, cot, att_t, d_t, terms)
    gain = gain_row + gain_term(xr, dh_col)
    terms[:, :, 4 * D :] = jnp.broadcast_to(gain, (128, D)).T.reshape(RANKS, 8, 128)

    def pack_core(b, carry):
        core_send[b] = terms[2 * b + 1 - core].astype(BF)
        return carry

    lax.fori_loop(0, RANKS // 2, pack_core, 0)
    pair = remote(core_send, core_recv, 3, {"seq": me + 1 - 2 * core})
    pair.start()
    pair.wait_recv()

    def pack_plane(b, carry):
        y, hi, x = b // 8, (b // 4) % 2, b % 4
        total = terms[2 * b + core] + core_recv[b].astype(F32)
        terms[2 * b + core] = total
        plane_send[y * 4 + x, hi] = total.astype(BF)
        return carry

    lax.fori_loop(0, RANKS // 2, pack_plane, 0)

    def send_plane(t, carry):
        other = lax.rem(plane + t, 16)
        remote(plane_send.at[other], plane_recv.at[plane], 4, {"seq": rank_of(other, z_hi)}).start()
        return carry

    lax.fori_loop(1, 16, send_plane, 0)

    own_h.wait()
    remote(dh_send.at[rest], dh_recv.at[rest], 2, {"seq": me}).wait_recv()

    def finish(i, carry):
        at = pl.multiple_of(i * CH, CH)
        inv, normed = norm_of(rows8(x_ref, i))
        grad_normed = (dh_row[pl.ds(at, CH), :] + rows8(dh_recv, i)) * g_ref[...]
        mean = jnp.mean(grad_normed * normed, -1, keepdims=True)
        grad = rows8(c_ref, i) + inv * (grad_normed - normed * mean)
        out_ref[pl.ds(i * (CH // 8), CH // 8)] = grad.astype(BF).reshape(CH // 8, 8, D)
        return carry

    lax.fori_loop(0, TOK // CH, finish, 0)

    pl_rest = pl.ds(0, 15)
    plane_in = remote(plane_send.at[pl_rest], plane_recv.at[pl_rest], 4, {"seq": me})
    plane_in.wait_recv()

    for hi in range(2):
        own_rank = (plane // 4) * 16 + hi * 8 + (plane % 4) * 2 + core
        z_sum[hi] = terms[own_rank]

        def add_plane(t, carry, hi=hi):
            other = lax.rem(plane + t, 16)
            z_sum[hi] += plane_recv[other, hi].astype(F32)
            return carry

        lax.fori_loop(1, 16, add_plane, 0)
        z_send[hi] = z_sum[hi].astype(BF)

    my_z = z_hi * LINE + line
    each_line_peer(
        lambda hi, lo: remote(
            z_send.at[hi], z_recv.at[my_z], 5, {"seq": rank_of(plane, hi), "dp": lo}
        ).start()
    )
    z_rest = pl.ds(0, 2 * LINE - 1)
    z_in = remote(z_recv.at[z_rest], z_recv.at[z_rest], 5, {"seq": me})
    z_in.wait_recv()
    z_sum[0] = z_sum[z_hi]

    def add_z(t, carry):
        z_sum[0] += z_recv[lax.rem(my_z + t, 2 * LINE)].astype(F32)
        return carry

    lax.fori_loop(1, 2 * LINE, add_z, 0)
    for part in range(3):
        gq_ref[:, part * D : part * D + HALF] = z_sum[0, :, part * HALF : (part + 1) * HALF]
        gq_ref[:, part * D + HALF : (part + 1) * D] = z_sum[0, :, (3 + part) * HALF : (4 + part) * HALF]
    go_ref[...] = z_sum[0, :, 3 * D : 4 * D]
    gg_ref[...] = z_sum[0, :, 4 * D :]

    in_x.wait_send()
    in_c.wait_send()
    remote(dh_send.at[rest], dh_recv.at[rest], 2, {"seq": me}).wait_send()
    pair.wait_send()
    plane_in.wait_send()
    z_in.wait_send()


def body(inputs, norm_gain, qkv_weight, out_weight, out_cotan):
    vmem = pl.BlockSpec(memory_space=pltpu.VMEM)
    grad, grad_qkv, grad_out, grad_gain = pl.pallas_call(
        kernel,
        out_shape=(
            jax.ShapeDtypeStruct((RANKS, 8, D), BF),
            jax.ShapeDtypeStruct((8, 3 * D), F32),
            jax.ShapeDtypeStruct((8, D), F32),
            jax.ShapeDtypeStruct((8, 128), F32),
        ),
        in_specs=[vmem] * 5,
        out_specs=(vmem,) * 4,
        scratch_shapes=[
            pltpu.VMEM((RANKS, 8, D), BF),
            pltpu.VMEM((RANKS, 8, D), BF),
            pltpu.VMEM((D, TOK), BF),
            pltpu.VMEM((TOK, D), BF),
            pltpu.VMEM((3 * HALF, TOK), BF),
            pltpu.VMEM((HALF, TOK), BF),
            pltpu.VMEM((HALF, TOK), BF),
            pltpu.VMEM((3 * HALF, TOK), BF),
            pltpu.VMEM((TOK, D), F32),
            pltpu.VMEM((TOK, D), F32),
            pltpu.VMEM((RANKS, 8, D), BF),
            pltpu.VMEM((RANKS, 8, D), BF),
            pltpu.VMEM((RANKS, 8, NC), F32),
            pltpu.VMEM((RANKS // 2, 8, NC), BF),
            pltpu.VMEM((RANKS // 2, 8, NC), BF),
            pltpu.VMEM((16, 2, 8, NC), BF),
            pltpu.VMEM((16, 2, 8, NC), BF),
            pltpu.VMEM((2, 8, NC), F32),
            pltpu.VMEM((2, 8, NC), BF),
            pltpu.VMEM((2 * LINE, 8, NC), BF),
            pltpu.SemaphoreType.DMA((6,)),
            pltpu.SemaphoreType.DMA((6,)),
            pltpu.SemaphoreType.DMA((2,)),
        ],
        compiler_params=pltpu.CompilerParams(
            collective_id=0, has_side_effects=True, vmem_limit_bytes=48 * 1024 * 1024
        ),
    )(
        inputs.reshape(RANKS, 8, D),
        out_cotan.reshape(RANKS, 8, D),
        norm_gain.reshape(1, D),
        qkv_weight,
        out_weight,
    )
    return (grad.reshape(inputs.shape), grad_qkv, grad_out, grad_gain[:, 0])


def solution(mesh):
    return jax.shard_map(
        body,
        mesh=mesh,
        in_specs=(P("dp", "seq", None, None), P(), P(), P(), P("dp", "seq", None, None)),
        out_specs=(P("dp", "seq", None, None), P("seq", None), P("seq", None), P("seq")),
        check_vma=False,
    )
```

```python
import jax
import jax.numpy as jnp
from jax import lax
from jax.experimental import pallas as pl
from jax.experimental.pallas import tpu as pltpu
from jax.sharding import PartitionSpec as P

MESH = pl.DeviceIdType.MESH
BF = jnp.bfloat16
F32 = jnp.float32
TOK = 512
D = 512
HALF = 256
HD = 64
RANKS = 64
LINE = 4
NC = 2048 + 128
PIECES = 4
CH = 128


def dot(a, b, ca, cb):
    return lax.dot_general(a, b, (((ca,), (cb,)), ((), ())), preferred_element_type=F32)


def rows8(ref, i):
    return ref[pl.ds(i * (CH // 8), CH // 8)].astype(F32).reshape(CH, D)


def norm_of(x):
    inv = lax.rsqrt(jnp.mean(x * x, -1, keepdims=True) + 1e-05)
    return inv, x * inv


def prepare_hidden(x_ref, g_ref, hid_t):
    def step(i, carry):
        _, normed = norm_of(rows8(x_ref, i))
        at = pl.multiple_of(i * CH, CH)
        hid_t[:, pl.ds(at, CH)] = (normed * g_ref[...]).T.astype(BF)
        return carry

    lax.fori_loop(0, TOK // CH, step, 0)


def project(w_ref, off, hid_t, qkv_t):
    for part in range(3):
        p = dot(w_ref[:, part * D + off : part * D + off + HALF], hid_t[...], 0, 0).astype(BF)
        if part == 0:
            p = p * BF(HD**-0.5)
        qkv_t[part * HALF : (part + 1) * HALF, :] = p


def prepare_cotangent(c_ref, wo_ref, off, cot, ga_t):
    def step(i, carry):
        at = pl.multiple_of(i * CH, CH)
        cot[pl.ds(at, CH), :] = rows8(c_ref, i).astype(BF)
        return carry

    lax.fori_loop(0, TOK // CH, step, 0)
    ga_t[...] = dot(wo_ref[off : off + HALF, :], cot[...], 1, 1).astype(BF)


def forward(is_col, qkv_t, att_t, probs):
    qb = TOK // 2

    def head(h, carry):
        at = pl.multiple_of(h * HD, HD)
        sl = pl.ds(at, HD)
        for b in range(2):
            kl = qb * (b + 1)
            qs = slice(b * qb, (b + 1) * qb)
            q = qkv_t[sl, qs]
            k = qkv_t[pl.ds(HALF + at, HD), :kl]
            v = qkv_t[pl.ds(2 * HALF + at, HD), :kl]
            s = dot(k, q, 0, 0)
            gap = (
                lax.broadcasted_iota(jnp.int32, (kl, qb), 1)
                + b * qb
                - lax.broadcasted_iota(jnp.int32, (kl, qb), 0)
            )
            allowed = gap >= 0
            if is_col:
                allowed = jnp.logical_and(allowed, jnp.bitwise_and(gap, 7) == 0)
            s = jnp.where(allowed, s, -1e30)
            e = jnp.exp(s - jnp.max(s, 0, keepdims=True))
            p = e * (1.0 / jnp.sum(e, 0, keepdims=True))
            probs[h, :kl, qs] = p
            att_t[sl, qs] = dot(v, p.astype(BF), 1, 0).astype(BF)
        return carry

    lax.fori_loop(0, HALF // HD, head, 0)


def backward(qkv_t, ga_t, att_t, probs, d_t):
    qb = TOK // 2

    def head(h, carry):
        at = pl.multiple_of(h * HD, HD)
        sl = pl.ds(at, HD)
        dk = dv = None
        for b in range(2):
            kl = qb * (b + 1)
            qs = slice(b * qb, (b + 1) * qb)
            q = qkv_t[sl, qs]
            k = qkv_t[pl.ds(HALF + at, HD), :kl]
            v = qkv_t[pl.ds(2 * HALF + at, HD), :kl]
            ga = ga_t[sl, qs]
            p = probs[h, :kl, qs]
            delta = jnp.sum(ga.astype(F32) * att_t[sl, qs].astype(F32), 0, keepdims=True)
            ds = (p * (dot(v, ga, 0, 0) - delta)).astype(BF)
            d_t[sl, qs] = (dot(k, ds, 1, 0) * (HD**-0.5)).astype(BF)
            dkb, dvb = dot(q, ds, 1, 1), dot(ga, p.astype(BF), 1, 1)
            if b == 0:
                dk, dv = dkb, dvb
            else:
                dk = jnp.concatenate([dk + dkb[:, :qb], dkb[:, qb:]], 1)
                dv = jnp.concatenate([dv + dvb[:, :qb], dvb[:, qb:]], 1)
        d_t[pl.ds(HALF + at, HD), :] = dk.astype(BF)
        d_t[pl.ds(2 * HALF + at, HD), :] = dv.astype(BF)
        return carry

    lax.fori_loop(0, HALF // HD, head, 0)


def hidden_grad(w_ref, off, d_t, dh):
    for part in range(3):
        d = d_t[part * HALF : (part + 1) * HALF, :]
        term = dot(d, w_ref[:, part * D + off : part * D + off + HALF], 0, 1)
        if part == 0:
            dh[...] = term
        else:
            dh[...] += term


def qkv_terms(hid_t, d_t, terms):
    for part in range(3):
        d = d_t[part * HALF : (part + 1) * HALF, :]
        at = part * HALF
        terms[:, :, at : at + HALF] = dot(hid_t[...], d, 1, 1).reshape(RANKS, 8, HALF)


def out_terms(off, cot, att_t, terms):
    half = slice(off // 8, (off + HALF) // 8)
    terms[half, :, 3 * HALF : 3 * HALF + D] = dot(att_t[...], cot[...], 1, 0).reshape(HALF // 8, 8, D)


def gain_term(x_ref, dh):
    def step(i, total):
        _, normed = norm_of(rows8(x_ref, i))
        at = pl.multiple_of(i * CH, CH)
        return total + jnp.sum(dh[pl.ds(at, CH), :] * normed, 0, keepdims=True)

    return lax.fori_loop(0, TOK // CH, step, jnp.zeros((1, D), F32))


def kernel(
    x_hbm, c_hbm, g_hbm, w_hbm, wo_hbm,
    out_hbm, gq_ref, go_ref, gg_ref,
    out_ref, x_ref, c_ref, g_ref, w_ref, wo_ref,
    xr, cr, hid_t, cot, qkv_t, ga_t, att_t, d_t, probs, dh_row, dh_col, dh_send, dh_recv,
    terms_a, core_send_a, core_recv_a, plane_send_a, plane_recv_a, z_sum_a, z_send_a, z_recv_a,
    terms_b, core_send_b, core_recv_b, plane_send_b, plane_recv_b, z_sum_b, z_send_b, z_recv_b,
    send_sem, recv_sem, own_sem,
):
    me = lax.axis_index("seq")
    line = lax.axis_index("dp")
    core = me % 2
    z_hi = (me // 8) % 2
    my_z = z_hi * LINE + line
    plane = (me // 16) * 4 + (me // 2) % 4
    early = (terms_a, core_send_a, core_recv_a, plane_send_a, plane_recv_a, z_sum_a, z_send_a, z_recv_a)
    late = (terms_b, core_send_b, core_recv_b, plane_send_b, plane_recv_b, z_sum_b, z_send_b, z_recv_b)

    def rank_of(other, hi):
        return (other // 4) * 16 + hi * 8 + (other % 4) * 2 + core

    def remote(src, dst, i, target):
        return pltpu.make_async_remote_copy(
            src, dst, send_sem.at[i], recv_sem.at[i], device_id=target, device_id_type=MESH
        )

    def each_peer(f):
        def step(t, carry):
            f(lax.rem(me + t, RANKS))
            return carry

        lax.fori_loop(1, RANKS, step, 0)

    loads = [
        pltpu.make_async_copy(src, dst, own_sem.at[i])
        for i, (src, dst) in enumerate(
            ((x_hbm, x_ref), (g_hbm, g_ref), (w_hbm, w_ref), (c_hbm, c_ref), (wo_hbm, wo_ref))
        )
    ]
    barrier = pltpu.get_barrier_semaphore()
    each_peer(lambda t: pl.semaphore_signal(barrier, inc=1, device_id={"seq": t}, device_id_type=MESH))
    for hi in range(2):
        for t in range(1, LINE):
            pl.semaphore_signal(
                barrier,
                inc=1,
                device_id={"seq": rank_of(plane, hi), "dp": lax.rem(line + t, LINE)},
                device_id_type=MESH,
            )
    for load in loads:
        load.start()
    pl.semaphore_wait(barrier, RANKS - 1 + 2 * (LINE - 1))

    each_peer(lambda t: remote(x_hbm.at[t], xr.at[me], 0, {"seq": t}).start())
    each_peer(lambda t: remote(c_hbm.at[t], cr.at[me], 1, {"seq": t}).start())
    for load in loads:
        load.wait()
    own_x = pltpu.make_async_copy(x_ref.at[me], xr.at[me], own_sem.at[0])
    own_c = pltpu.make_async_copy(c_ref.at[me], cr.at[me], own_sem.at[1])
    own_x.start()
    own_c.start()
    rest = pl.ds(0, RANKS - 1)
    in_x = remote(x_hbm.at[rest], xr.at[rest], 0, {"seq": me})
    in_c = remote(c_hbm.at[rest], cr.at[rest], 1, {"seq": me})

    def core_phase(bufs, i):
        terms, core_send, core_recv = bufs[:3]

        def pack(b, carry):
            core_send[b] = terms[2 * b + 1 - core].astype(BF)
            return carry

        lax.fori_loop(0, RANKS // 2, pack, 0)
        pair = remote(core_send, core_recv, i, {"seq": me + 1 - 2 * core})
        pair.start()
        return pair

    def plane_phase(bufs, i, pair):
        terms, _, core_recv, plane_send, plane_recv = bufs[:5]
        pair.wait_recv()

        def pack(b, carry):
            y, hi, x = b // 8, (b // 4) % 2, b % 4
            total = terms[2 * b + core] + core_recv[b].astype(F32)
            terms[2 * b + core] = total
            plane_send[y * 4 + x, hi] = total.astype(BF)
            return carry

        lax.fori_loop(0, RANKS // 2, pack, 0)

        def send(t, carry):
            other = lax.rem(plane + t, 16)
            remote(plane_send.at[other], plane_recv.at[plane], i, {"seq": rank_of(other, z_hi)}).start()
            return carry

        lax.fori_loop(1, 16, send, 0)
        others = pl.ds(0, 15)
        return remote(plane_send.at[others], plane_recv.at[others], i, {"seq": me})

    def z_phase(bufs, i, plane_in):
        terms, _, _, _, plane_recv, z_sum, z_send, z_recv = bufs
        plane_in.wait_recv()
        for hi in range(2):
            own = terms[rank_of(plane, hi)]

            def add(t, total, hi=hi):
                return total + plane_recv[lax.rem(plane + t, 16), hi].astype(F32)

            total = lax.fori_loop(1, 16, add, own)
            z_sum[hi] = total
            z_send[hi] = total.astype(BF)

        def send(t, carry):
            z = lax.rem(my_z + t, 2 * LINE)
            hi = z // LINE
            remote(z_send.at[hi], z_recv.at[my_z], i, {"seq": rank_of(plane, hi), "dp": z % LINE}).start()
            return carry

        lax.fori_loop(1, 2 * LINE, send, 0)
        others = pl.ds(0, 2 * LINE - 1)
        return remote(z_recv.at[others], z_recv.at[others], i, {"seq": me})

    def z_total(bufs, z_in):
        z_sum, _, z_recv = bufs[5:]
        z_in.wait_recv()

        def add(t, total):
            return total + z_recv[lax.rem(my_z + t, 2 * LINE)].astype(F32)

        return lax.fori_loop(1, 2 * LINE, add, z_sum[z_hi])

    prepare_hidden(x_ref, g_ref, hid_t)
    project(w_ref, 0, hid_t, qkv_t)
    forward(False, qkv_t, att_t, probs)
    prepare_cotangent(c_ref, wo_ref, 0, cot, ga_t)
    backward(qkv_t, ga_t, att_t, probs, d_t)
    qkv_terms(hid_t, d_t, terms_a)
    pair_a = core_phase(early, 3)
    hidden_grad(w_ref, 0, d_t, dh_row)
    out_terms(0, cot, att_t, terms_b)
    gain_row = gain_term(x_ref, dh_row)
    plane_a = plane_phase(early, 4, pair_a)

    own_x.wait()
    in_x.wait_recv()
    prepare_hidden(xr, g_ref, hid_t)
    project(w_ref, HALF, hid_t, qkv_t)
    forward(True, qkv_t, att_t, probs)
    own_c.wait()
    in_c.wait_recv()
    prepare_cotangent(cr, wo_ref, HALF, cot, ga_t)
    backward(qkv_t, ga_t, att_t, probs, d_t)
    hidden_grad(w_ref, HALF, d_t, dh_col)

    def round_out(i, carry):
        at = pl.multiple_of(i * CH, CH)
        dh_send[pl.ds(i * (CH // 8), CH // 8)] = dh_col[pl.ds(at, CH), :].reshape(CH // 8, 8, D).astype(BF)
        return carry

    lax.fori_loop(0, TOK // CH, round_out, 0)
    each_peer(lambda t: remote(dh_send.at[t], dh_recv.at[me], 2, {"seq": t}).start())
    own_h = pltpu.make_async_copy(dh_send.at[me], dh_recv.at[me], own_sem.at[0])
    own_h.start()
    out_in = remote(dh_send.at[rest], dh_recv.at[rest], 2, {"seq": me})

    qkv_terms(hid_t, d_t, terms_b)
    out_terms(HALF, cot, att_t, terms_b)
    gain = gain_row + gain_term(xr, dh_col)
    terms_b[:, :, 3 * HALF + D :] = jnp.broadcast_to(gain, (128, D)).T.reshape(RANKS, 8, 128)
    pair_b = core_phase(late, 6)
    z_a = z_phase(early, 5, plane_a)
    plane_b = plane_phase(late, 7, pair_b)

    own_h.wait()
    out_in.wait_recv()

    def finish(i, carry):
        at = pl.multiple_of(i * CH, CH)
        inv, normed = norm_of(rows8(x_ref, i))
        grad_normed = (dh_row[pl.ds(at, CH), :] + rows8(dh_recv, i)) * g_ref[...]
        mean = jnp.mean(grad_normed * normed, -1, keepdims=True)
        grad = rows8(c_ref, i) + inv * (grad_normed - normed * mean)
        out_ref[pl.ds(i * (CH // 8), CH // 8)] = grad.astype(BF).reshape(CH // 8, 8, D)
        return carry

    lax.fori_loop(0, TOK // CH, finish, 0)
    out_copy = pltpu.make_async_copy(out_ref, out_hbm, own_sem.at[1])
    out_copy.start()

    z_b = z_phase(late, 8, plane_b)
    total_a = z_total(early, z_a)
    total_b = z_total(late, z_b)
    for part in range(3):
        gq_ref[:, part * D : part * D + HALF] = total_a[:, part * HALF : (part + 1) * HALF]
        gq_ref[:, part * D + HALF : (part + 1) * D] = total_b[:, part * HALF : (part + 1) * HALF]
    go_ref[...] = total_b[:, 3 * HALF : 3 * HALF + D]
    gg_ref[...] = total_b[:, 3 * HALF + D :]

    out_copy.wait()
    for copy in (in_x, in_c, out_in, pair_a, plane_a, z_a, pair_b, plane_b, z_b):
        copy.wait_send()


def deliver(grad, gq, go, gg, grad_out, gq_out, go_out, gg_out, grad_v, gq_v, go_v, gg_v, gain, sem):
    step = RANKS // PIECES
    moves = [(gg, gg_v, gg_out), (gq, gq_v, gq_out), (go, go_v, go_out)]
    moves += [
        tuple(r.at[pl.ds(i * step, step)] for r in (grad, grad_v, grad_out)) for i in range(PIECES)
    ]
    loads = [pltpu.make_async_copy(a, b, sem.at[0, i]) for i, (a, b, _) in enumerate(moves)]
    for load in loads:
        load.start()
    stores = []
    for i, (_, b, c) in enumerate(moves):
        loads[i].wait()
        if i == 0:
            rows = lax.broadcasted_iota(jnp.int32, (8, 128), 0)
            lanes = lax.broadcasted_iota(jnp.int32, (8, 128), 1)
            gain[...] = jnp.sum(jnp.where(rows == lanes, gg_v[...], 0.0), 0, keepdims=True)[:, :8]
            b = gain
        stores.append(pltpu.make_async_copy(b, c, sem.at[1, i]))
        stores[-1].start()
    for store in stores:
        store.wait()


def sum_buffers(cols):
    return [
        pltpu.VMEM((RANKS, 8, cols), F32),
        pltpu.VMEM((RANKS // 2, 8, cols), BF),
        pltpu.VMEM((RANKS // 2, 8, cols), BF),
        pltpu.VMEM((16, 2, 8, cols), BF),
        pltpu.VMEM((16, 2, 8, cols), BF),
        pltpu.VMEM((2, 8, cols), F32),
        pltpu.VMEM((2, 8, cols), BF),
        pltpu.VMEM((2 * LINE, 8, cols), BF),
    ]


def body(inputs, norm_gain, qkv_weight, out_weight, out_cotan):
    vmem = pl.BlockSpec(memory_space=pltpu.VMEM)
    hbm = pl.BlockSpec(memory_space=pl.ANY)
    shapes = (
        jax.ShapeDtypeStruct((RANKS, 8, D), BF),
        jax.ShapeDtypeStruct((8, 3 * D), F32),
        jax.ShapeDtypeStruct((8, D), F32),
    )
    results = pl.pallas_call(
        kernel,
        out_shape=shapes + (jax.ShapeDtypeStruct((8, 128), F32),),
        in_specs=[hbm] * 5,
        out_specs=(hbm, vmem, vmem, vmem),
        scratch_shapes=[
            pltpu.VMEM((RANKS, 8, D), BF),
            pltpu.VMEM((RANKS, 8, D), BF),
            pltpu.VMEM((RANKS, 8, D), BF),
            pltpu.VMEM((1, D), F32),
            pltpu.VMEM((D, 3 * D), BF),
            pltpu.VMEM((D, D), BF),
            pltpu.VMEM((RANKS, 8, D), BF),
            pltpu.VMEM((RANKS, 8, D), BF),
            pltpu.VMEM((D, TOK), BF),
            pltpu.VMEM((TOK, D), BF),
            pltpu.VMEM((3 * HALF, TOK), BF),
            pltpu.VMEM((HALF, TOK), BF),
            pltpu.VMEM((HALF, TOK), BF),
            pltpu.VMEM((3 * HALF, TOK), BF),
            pltpu.VMEM((HALF // HD, TOK, TOK), F32),
            pltpu.VMEM((TOK, D), F32),
            pltpu.VMEM((TOK, D), F32),
            pltpu.VMEM((RANKS, 8, D), BF),
            pltpu.VMEM((RANKS, 8, D), BF),
            *sum_buffers(3 * HALF),
            *sum_buffers(3 * HALF + D + 128),
            pltpu.SemaphoreType.DMA((9,)),
            pltpu.SemaphoreType.DMA((9,)),
            pltpu.SemaphoreType.DMA((5,)),
        ],
        compiler_params=pltpu.CompilerParams(
            collective_id=0, has_side_effects=True, vmem_limit_bytes=60 * 1024 * 1024
        ),
    )(
        inputs.reshape(RANKS, 8, D),
        out_cotan.reshape(RANKS, 8, D),
        norm_gain.reshape(1, D),
        qkv_weight,
        out_weight,
    )
    grad, grad_qkv, grad_out, grad_gain = pl.pallas_call(
        deliver,
        out_shape=shapes + (jax.ShapeDtypeStruct((1, 8), F32),),
        in_specs=[hbm] * 4,
        out_specs=(hbm,) * 4,
        scratch_shapes=[
            pltpu.VMEM((RANKS, 8, D), BF),
            pltpu.VMEM((8, 3 * D), F32),
            pltpu.VMEM((8, D), F32),
            pltpu.VMEM((8, 128), F32),
            pltpu.VMEM((1, 8), F32),
            pltpu.SemaphoreType.DMA((2, 3 + PIECES)),
        ],
    )(*results)
    return (grad.reshape(inputs.shape), grad_qkv, grad_out, grad_gain.reshape(8))


def solution(mesh):
    return jax.shard_map(
        body,
        mesh=mesh,
        in_specs=(P("dp", "seq", None, None), P(), P(), P(), P("dp", "seq", None, None)),
        out_specs=(P("dp", "seq", None, None), P("seq", None), P("seq", None), P("seq")),
        check_vma=False,
    )
```

```python
import jax
import jax.numpy as jnp
from jax import lax
from jax.experimental import pallas as pl
from jax.experimental.pallas import tpu as pltpu
from jax.sharding import PartitionSpec as P

MESH = pl.DeviceIdType.MESH
BF = jnp.bfloat16
F32 = jnp.float32
TOK = 512
D = 512
HALF = 256
HD = 64
RANKS = 64
LINE = 4
PIECES = 4
CH = 128


def dot(a, b, ca, cb):
    return lax.dot_general(a, b, (((ca,), (cb,)), ((), ())), preferred_element_type=F32)


def rows8(ref, i):
    return ref[pl.ds(i * (CH // 8), CH // 8)].astype(F32).reshape(CH, D)


def norm_of(x):
    inv = lax.rsqrt(jnp.mean(x * x, -1, keepdims=True) + 1e-05)
    return inv, x * inv


def prepare_hidden(x_ref, g_ref, hid_t):
    def step(i, carry):
        _, normed = norm_of(rows8(x_ref, i))
        at = pl.multiple_of(i * CH, CH)
        hid_t[:, pl.ds(at, CH)] = (normed * g_ref[...]).T.astype(BF)
        return carry

    lax.fori_loop(0, TOK // CH, step, 0)


def project(w_ref, off, hid_t, qkv_t):
    for part in range(3):
        p = dot(w_ref[:, part * D + off : part * D + off + HALF], hid_t[...], 0, 0).astype(BF)
        if part == 0:
            p = p * BF(HD**-0.5)
        qkv_t[part * HALF : (part + 1) * HALF, :] = p


def prepare_cotangent(c_ref, wo_ref, off, cot, ga_t):
    def step(i, carry):
        at = pl.multiple_of(i * CH, CH)
        cot[pl.ds(at, CH), :] = rows8(c_ref, i).astype(BF)
        return carry

    lax.fori_loop(0, TOK // CH, step, 0)
    ga_t[...] = dot(wo_ref[off : off + HALF, :], cot[...], 1, 1).astype(BF)


def forward(is_col, qkv_t, att_t, probs):
    qb = TOK // 2

    def head(h, carry):
        at = pl.multiple_of(h * HD, HD)
        sl = pl.ds(at, HD)
        for b in range(2):
            kl = qb * (b + 1)
            qs = slice(b * qb, (b + 1) * qb)
            q = qkv_t[sl, qs]
            k = qkv_t[pl.ds(HALF + at, HD), :kl]
            v = qkv_t[pl.ds(2 * HALF + at, HD), :kl]
            s = dot(k, q, 0, 0)
            gap = (
                lax.broadcasted_iota(jnp.int32, (kl, qb), 1)
                + b * qb
                - lax.broadcasted_iota(jnp.int32, (kl, qb), 0)
            )
            allowed = gap >= 0
            if is_col:
                allowed = jnp.logical_and(allowed, jnp.bitwise_and(gap, 7) == 0)
            s = jnp.where(allowed, s, -1e30)
            e = jnp.exp(s - jnp.max(s, 0, keepdims=True))
            p = e * (1.0 / jnp.sum(e, 0, keepdims=True))
            probs[h, :kl, qs] = p
            att_t[sl, qs] = dot(v, p.astype(BF), 1, 0).astype(BF)
        return carry

    lax.fori_loop(0, HALF // HD, head, 0)


def backward(first, last, qkv_t, ga_t, att_t, probs, d_t):
    qb = TOK // 2

    def head(h, carry):
        at = pl.multiple_of(h * HD, HD)
        sl = pl.ds(at, HD)
        dk = dv = None
        for b in range(2):
            kl = qb * (b + 1)
            qs = slice(b * qb, (b + 1) * qb)
            q = qkv_t[sl, qs]
            k = qkv_t[pl.ds(HALF + at, HD), :kl]
            v = qkv_t[pl.ds(2 * HALF + at, HD), :kl]
            ga = ga_t[sl, qs]
            p = probs[h, :kl, qs]
            delta = jnp.sum(ga.astype(F32) * att_t[sl, qs].astype(F32), 0, keepdims=True)
            ds = (p * (dot(v, ga, 0, 0) - delta)).astype(BF)
            d_t[sl, qs] = (dot(k, ds, 1, 0) * (HD**-0.5)).astype(BF)
            dkb, dvb = dot(q, ds, 1, 1), dot(ga, p.astype(BF), 1, 1)
            if b == 0:
                dk, dv = dkb, dvb
            else:
                dk = jnp.concatenate([dk + dkb[:, :qb], dkb[:, qb:]], 1)
                dv = jnp.concatenate([dv + dvb[:, :qb], dvb[:, qb:]], 1)
        d_t[pl.ds(HALF + at, HD), :] = dk.astype(BF)
        d_t[pl.ds(2 * HALF + at, HD), :] = dv.astype(BF)
        return carry

    lax.fori_loop(first, last, head, 0)


def hidden_grad(w_ref, off, d_t, dh):
    for part in range(3):
        d = d_t[part * HALF : (part + 1) * HALF, :]
        term = dot(d, w_ref[:, part * D + off : part * D + off + HALF], 0, 1)
        if part == 0:
            dh[...] = term
        else:
            dh[...] += term


def qkv_terms(hid_t, d_t, terms):
    for part in range(3):
        d = d_t[part * HALF : (part + 1) * HALF, :]
        at = part * HALF
        terms[:, :, :, at : at + HALF] = dot(hid_t[...], d, 1, 1).reshape(RANKS // 2, 2, 8, HALF)


def out_terms(off, cot, att_t, terms):
    half = slice(off // 16, (off + HALF) // 16)
    terms[half] = dot(att_t[...], cot[...], 1, 0).reshape(HALF // 16, 2, 8, D)


def gain_term(x_ref, dh):
    def step(i, total):
        _, normed = norm_of(rows8(x_ref, i))
        at = pl.multiple_of(i * CH, CH)
        return total + jnp.sum(dh[pl.ds(at, CH), :] * normed, 0, keepdims=True)

    return lax.fori_loop(0, TOK // CH, step, jnp.zeros((1, D), F32))


def kernel(
    x_hbm, c_hbm, g_hbm, w_hbm, wo_hbm,
    out_hbm, gq_ref, go_ref, gg_ref,
    out_ref, x_ref, c_ref, g_ref, w_ref, wo_ref,
    xr, cr, hid_t, cot, qkv_t, ga_t, att_t, d_t, probs, dh_row, dh_col, dh_send, dh_recv,
    terms_a, core_send_a, core_recv_a, plane_send_a, plane_recv_a, z_sum_a, z_send_a, z_recv_a,
    terms_b, core_send_b, core_recv_b, plane_send_b, plane_recv_b, z_sum_b, z_send_b, z_recv_b,
    terms_c, core_send_c, core_recv_c, plane_send_c, plane_recv_c, z_sum_c, z_send_c, z_recv_c,
    gain_core, gain_pair, gain_plane, gain_planes, gain_z, gain_zs,
    send_sem, recv_sem, own_sem,
):
    me = lax.axis_index("seq")
    line = lax.axis_index("dp")
    core = me % 2
    z_hi = (me // 8) % 2
    my_z = z_hi * LINE + line
    plane = (me // 16) * 4 + (me // 2) % 4
    early = (terms_a, core_send_a, core_recv_a, plane_send_a, plane_recv_a, z_sum_a, z_send_a, z_recv_a)
    middle = (terms_b, core_send_b, core_recv_b, plane_send_b, plane_recv_b, z_sum_b, z_send_b, z_recv_b)
    late = (terms_c, core_send_c, core_recv_c, plane_send_c, plane_recv_c, z_sum_c, z_send_c, z_recv_c)

    def rank_of(other, hi):
        return (other // 4) * 16 + hi * 8 + (other % 4) * 2 + core

    def remote(src, dst, i, target):
        return pltpu.make_async_remote_copy(
            src, dst, send_sem.at[i], recv_sem.at[i], device_id=target, device_id_type=MESH
        )

    def each_peer(f):
        def step(i, carry):
            for t in range(7):
                f(lax.rem(me + 1 + i * 7 + t, RANKS))
            return carry

        lax.fori_loop(0, (RANKS - 1) // 7, step, 0)

    loads = [
        pltpu.make_async_copy(src, dst, own_sem.at[i])
        for i, (src, dst) in enumerate(
            ((x_hbm, x_ref), (g_hbm, g_ref), (w_hbm, w_ref), (c_hbm, c_ref), (wo_hbm, wo_ref))
        )
    ]
    barrier = pltpu.get_barrier_semaphore()
    each_peer(lambda t: pl.semaphore_signal(barrier, inc=1, device_id={"seq": t}, device_id_type=MESH))
    for hi in range(2):
        for t in range(1, LINE):
            pl.semaphore_signal(
                barrier,
                inc=1,
                device_id={"seq": rank_of(plane, hi), "dp": lax.rem(line + t, LINE)},
                device_id_type=MESH,
            )
    for load in loads:
        load.start()
    pl.semaphore_wait(barrier, RANKS - 1 + 2 * (LINE - 1))

    each_peer(lambda t: remote(x_hbm.at[t], xr.at[me], 0, {"seq": t}).start())
    each_peer(lambda t: remote(c_hbm.at[t], cr.at[me], 1, {"seq": t}).start())
    for load in loads:
        load.wait()
    own_x = pltpu.make_async_copy(x_ref.at[me], xr.at[me], own_sem.at[0])
    own_c = pltpu.make_async_copy(c_ref.at[me], cr.at[me], own_sem.at[1])
    own_x.start()
    own_c.start()
    rest = pl.ds(0, RANKS - 1)
    in_x = remote(x_hbm.at[rest], xr.at[rest], 0, {"seq": me})
    in_c = remote(c_hbm.at[rest], cr.at[rest], 1, {"seq": me})

    def core_phase(bufs, i):
        terms, core_send, core_recv = bufs[:3]
        core_send[...] = terms[:, 1 - core].astype(BF)
        pair = remote(core_send, core_recv, i, {"seq": me + 1 - 2 * core})
        pair.start()
        return pair

    def plane_phase(bufs, i, pair):
        terms, _, core_recv, plane_send, plane_recv = bufs[:5]
        pair.wait_recv()
        plane_send[...] = (terms[:, core] + core_recv[...].astype(F32)).astype(BF).reshape(plane_send.shape)
        for t in range(1, 16):
            other = lax.rem(plane + t, 16)
            remote(
                plane_send.at[other // 4, :, other % 4],
                plane_recv.at[plane],
                i,
                {"seq": rank_of(other, z_hi)},
            ).start()
        others = plane_recv.at[pl.ds(0, 15)]
        return remote(others, others, i, {"seq": me})

    def z_phase(bufs, i, plane_in):
        terms, _, core_recv, _, plane_recv, z_sum, z_send, z_recv = bufs
        plane_in.wait_recv()
        for hi in range(2):
            own = rank_of(plane, hi) // 2
            total = terms[own, core] + core_recv[own].astype(F32)
            for t in range(1, 16):
                total += plane_recv[lax.rem(plane + t, 16), hi].astype(F32)
            z_sum[hi] = total
            z_send[hi] = total.astype(BF)
        for t in range(1, 2 * LINE):
            z = lax.rem(my_z + t, 2 * LINE)
            hi = z // LINE
            remote(z_send.at[hi], z_recv.at[my_z], i, {"seq": rank_of(plane, hi), "dp": z % LINE}).start()
        others = z_recv.at[pl.ds(0, 2 * LINE - 1)]
        return remote(others, others, i, {"seq": me})

    def z_total(bufs, z_in):
        z_sum, _, z_recv = bufs[5:]
        z_in.wait_recv()
        total = z_sum[z_hi]
        for t in range(1, 2 * LINE):
            total += z_recv[lax.rem(my_z + t, 2 * LINE)].astype(F32)
        return total

    def gain_plane_phase(pair):
        pair.wait_recv()
        gain_plane[...] = gain_core[...] + gain_pair[...]
        for t in range(1, 16):
            to = rank_of(lax.rem(plane + t, 16), z_hi)
            remote(gain_plane, gain_planes.at[plane], 12, {"seq": to}).start()
        others = gain_planes.at[pl.ds(0, 15)]
        return remote(others, others, 12, {"seq": me})

    def gain_z_phase(plane_in):
        plane_in.wait_recv()
        total = gain_plane[...]
        for t in range(1, 16):
            total += gain_planes[lax.rem(plane + t, 16)]
        gain_z[...] = total
        for t in range(1, 2 * LINE):
            z = lax.rem(my_z + t, 2 * LINE)
            to = {"seq": rank_of(plane, z // LINE), "dp": z % LINE}
            remote(gain_z, gain_zs.at[my_z], 13, to).start()
        others = gain_zs.at[pl.ds(0, 2 * LINE - 1)]
        return remote(others, others, 13, {"seq": me})

    prepare_hidden(x_ref, g_ref, hid_t)
    project(w_ref, 0, hid_t, qkv_t)
    forward(False, qkv_t, att_t, probs)
    prepare_cotangent(c_ref, wo_ref, 0, cot, ga_t)
    backward(0, 4, qkv_t, ga_t, att_t, probs, d_t)
    qkv_terms(hid_t, d_t, terms_a)
    pair_a = core_phase(early, 3)
    hidden_grad(w_ref, 0, d_t, dh_row)
    out_terms(0, cot, att_t, terms_b)
    gain_row = gain_term(x_ref, dh_row)
    plane_a = plane_phase(early, 4, pair_a)

    own_x.wait()
    in_x.wait_recv()
    prepare_hidden(xr, g_ref, hid_t)
    project(w_ref, HALF, hid_t, qkv_t)
    forward(True, qkv_t, att_t, probs)
    own_c.wait()
    in_c.wait_recv()
    prepare_cotangent(cr, wo_ref, HALF, cot, ga_t)
    out_terms(HALF, cot, att_t, terms_b)
    pair_b = core_phase(middle, 6)
    z_a = z_phase(early, 5, plane_a)
    backward(0, 2, qkv_t, ga_t, att_t, probs, d_t)
    plane_b = plane_phase(middle, 7, pair_b)
    backward(2, 4, qkv_t, ga_t, att_t, probs, d_t)
    hidden_grad(w_ref, HALF, d_t, dh_col)

    def round_out(i, carry):
        at = pl.multiple_of(i * CH, CH)
        dh_send[pl.ds(i * (CH // 8), CH // 8)] = dh_col[pl.ds(at, CH), :].reshape(CH // 8, 8, D).astype(BF)
        return carry

    lax.fori_loop(0, TOK // CH, round_out, 0)
    each_peer(lambda t: remote(dh_send.at[t], dh_recv.at[me], 2, {"seq": t}).start())
    own_h = pltpu.make_async_copy(dh_send.at[me], dh_recv.at[me], own_sem.at[0])
    own_h.start()
    out_in = remote(dh_send.at[rest], dh_recv.at[rest], 2, {"seq": me})

    qkv_terms(hid_t, d_t, terms_c)
    pair_c = core_phase(late, 9)
    gain = gain_row + gain_term(xr, dh_col)
    gain_core[...] = jnp.zeros((8, 128), F32)
    for i in range(D // 128):
        gain_core[i : i + 1, :] = gain[:, i * 128 : (i + 1) * 128]
    pair_g = remote(gain_core, gain_pair, 14, {"seq": me + 1 - 2 * core})
    pair_g.start()
    plane_c = plane_phase(late, 10, pair_c)
    z_b = z_phase(middle, 8, plane_b)
    plane_g = gain_plane_phase(pair_g)
    z_c = z_phase(late, 11, plane_c)
    z_g = gain_z_phase(plane_g)

    own_h.wait()
    out_in.wait_recv()

    def finish(i, carry):
        at = pl.multiple_of(i * CH, CH)
        inv, normed = norm_of(rows8(x_ref, i))
        grad_normed = (dh_row[pl.ds(at, CH), :] + rows8(dh_recv, i)) * g_ref[...]
        mean = jnp.mean(grad_normed * normed, -1, keepdims=True)
        grad = rows8(c_ref, i) + inv * (grad_normed - normed * mean)
        out_ref[pl.ds(i * (CH // 8), CH // 8)] = grad.astype(BF).reshape(CH // 8, 8, D)
        return carry

    lax.fori_loop(0, TOK // CH, finish, 0)
    out_copy = pltpu.make_async_copy(out_ref, out_hbm, own_sem.at[1])
    out_copy.start()

    total_a = z_total(early, z_a)
    go_ref[...] = z_total(middle, z_b)
    total_c = z_total(late, z_c)
    for part in range(3):
        gq_ref[:, part * D : part * D + HALF] = total_a[:, part * HALF : (part + 1) * HALF]
        gq_ref[:, part * D + HALF : (part + 1) * D] = total_c[:, part * HALF : (part + 1) * HALF]
    z_g.wait_recv()

    total_g = gain_z[...]
    for t in range(1, 2 * LINE):
        total_g += gain_zs[lax.rem(my_z + t, 2 * LINE)]
    rows = lax.broadcasted_iota(jnp.int32, (8, 128), 0)
    lanes = lax.broadcasted_iota(jnp.int32, (8, 128), 1)
    mine = jnp.sum(jnp.where(rows == me // 16, total_g, 0.0), 0, keepdims=True)
    picked = jnp.where(lanes == (me % 16) * 8 + rows, mine, 0.0)
    gg_ref[...] = jnp.broadcast_to(jnp.sum(picked, 1, keepdims=True), (8, 128))

    out_copy.wait()
    sums = (pair_a, plane_a, z_a, pair_b, plane_b, z_b, pair_c, plane_c, z_c, pair_g, plane_g, z_g)
    for copy in (in_x, in_c, out_in, *sums):
        copy.wait_send()


def deliver(grad, gq, go, gg, grad_out, gq_out, go_out, gg_out, grad_v, gq_v, go_v, gg_v, gain, sem):
    step = RANKS // PIECES
    moves = [(gg, gg_v, gg_out), (gq, gq_v, gq_out), (go, go_v, go_out)]
    moves += [
        tuple(r.at[pl.ds(i * step, step)] for r in (grad, grad_v, grad_out)) for i in range(PIECES)
    ]
    loads = [pltpu.make_async_copy(a, b, sem.at[0, i]) for i, (a, b, _) in enumerate(moves)]
    for load in loads:
        load.start()
    stores = []
    for i, (_, b, c) in enumerate(moves):
        loads[i].wait()
        if i == 0:
            rows = lax.broadcasted_iota(jnp.int32, (8, 128), 0)
            lanes = lax.broadcasted_iota(jnp.int32, (8, 128), 1)
            gain[...] = jnp.sum(jnp.where(rows == lanes, gg_v[...], 0.0), 0, keepdims=True)[:, :8]
            b = gain
        stores.append(pltpu.make_async_copy(b, c, sem.at[1, i]))
        stores[-1].start()
    for store in stores:
        store.wait()


def sum_buffers(cols):
    return [
        pltpu.VMEM((RANKS // 2, 2, 8, cols), F32),
        pltpu.VMEM((RANKS // 2, 8, cols), BF),
        pltpu.VMEM((RANKS // 2, 8, cols), BF),
        pltpu.VMEM((4, 2, 4, 8, cols), BF),
        pltpu.VMEM((16, 2, 8, cols), BF),
        pltpu.VMEM((2, 8, cols), F32),
        pltpu.VMEM((2, 8, cols), BF),
        pltpu.VMEM((2 * LINE, 8, cols), BF),
    ]


def body(inputs, norm_gain, qkv_weight, out_weight, out_cotan):
    vmem = pl.BlockSpec(memory_space=pltpu.VMEM)
    hbm = pl.BlockSpec(memory_space=pl.ANY)
    shapes = (
        jax.ShapeDtypeStruct((RANKS, 8, D), BF),
        jax.ShapeDtypeStruct((8, 3 * D), F32),
        jax.ShapeDtypeStruct((8, D), F32),
    )
    results = pl.pallas_call(
        kernel,
        out_shape=shapes + (jax.ShapeDtypeStruct((8, 128), F32),),
        in_specs=[hbm] * 5,
        out_specs=(hbm, vmem, vmem, vmem),
        scratch_shapes=[
            pltpu.VMEM((RANKS, 8, D), BF),
            pltpu.VMEM((RANKS, 8, D), BF),
            pltpu.VMEM((RANKS, 8, D), BF),
            pltpu.VMEM((1, D), F32),
            pltpu.VMEM((D, 3 * D), BF),
            pltpu.VMEM((D, D), BF),
            pltpu.VMEM((RANKS, 8, D), BF),
            pltpu.VMEM((RANKS, 8, D), BF),
            pltpu.VMEM((D, TOK), BF),
            pltpu.VMEM((TOK, D), BF),
            pltpu.VMEM((3 * HALF, TOK), BF),
            pltpu.VMEM((HALF, TOK), BF),
            pltpu.VMEM((HALF, TOK), BF),
            pltpu.VMEM((3 * HALF, TOK), BF),
            pltpu.VMEM((HALF // HD, TOK, TOK), F32),
            pltpu.VMEM((TOK, D), F32),
            pltpu.VMEM((TOK, D), F32),
            pltpu.VMEM((RANKS, 8, D), BF),
            pltpu.VMEM((RANKS, 8, D), BF),
            *sum_buffers(3 * HALF),
            *sum_buffers(D),
            *sum_buffers(3 * HALF),
            pltpu.VMEM((8, 128), F32),
            pltpu.VMEM((8, 128), F32),
            pltpu.VMEM((8, 128), F32),
            pltpu.VMEM((16, 8, 128), F32),
            pltpu.VMEM((8, 128), F32),
            pltpu.VMEM((2 * LINE, 8, 128), F32),
            pltpu.SemaphoreType.DMA((15,)),
            pltpu.SemaphoreType.DMA((15,)),
            pltpu.SemaphoreType.DMA((5,)),
        ],
        compiler_params=pltpu.CompilerParams(
            collective_id=0, has_side_effects=True, vmem_limit_bytes=60 * 1024 * 1024
        ),
    )(
        inputs.reshape(RANKS, 8, D),
        out_cotan.reshape(RANKS, 8, D),
        norm_gain.reshape(1, D),
        qkv_weight,
        out_weight,
    )
    grad, grad_qkv, grad_out, grad_gain = pl.pallas_call(
        deliver,
        out_shape=shapes + (jax.ShapeDtypeStruct((1, 8), F32),),
        in_specs=[hbm] * 4,
        out_specs=(hbm,) * 4,
        scratch_shapes=[
            pltpu.VMEM((RANKS, 8, D), BF),
            pltpu.VMEM((8, 3 * D), F32),
            pltpu.VMEM((8, D), F32),
            pltpu.VMEM((8, 128), F32),
            pltpu.VMEM((1, 8), F32),
            pltpu.SemaphoreType.DMA((2, 3 + PIECES)),
        ],
    )(*results)
    return (grad.reshape(inputs.shape), grad_qkv, grad_out, grad_gain.reshape(8))


def solution(mesh):
    return jax.shard_map(
        body,
        mesh=mesh,
        in_specs=(P("dp", "seq", None, None), P(), P(), P(), P("dp", "seq", None, None)),
        out_specs=(P("dp", "seq", None, None), P("seq", None), P("seq", None), P("seq")),
        check_vma=False,
    )
```

```python
import jax
import jax.numpy as jnp
from jax import lax
from jax.experimental import pallas as pl
from jax.experimental.pallas import tpu as pltpu
from jax.sharding import PartitionSpec as P

MESH = pl.DeviceIdType.MESH
BF = jnp.bfloat16
F32 = jnp.float32
TOK = 512
D = 512
HALF = 256
HD = 64
RANKS = 64
LINE = 4
PIECES = 4
CH = 128


def dot(a, b, ca, cb):
    return lax.dot_general(a, b, (((ca,), (cb,)), ((), ())), preferred_element_type=F32)


def rows8(ref, i):
    return ref[pl.ds(i * (CH // 8), CH // 8)].astype(F32).reshape(CH, D)


def norm_of(x):
    inv = lax.rsqrt(jnp.mean(x * x, -1, keepdims=True) + 1e-05)
    return inv, x * inv


def prepare_hidden(x_ref, g_ref, hid_t, keep=None):
    def step(i, carry):
        inv, normed = norm_of(rows8(x_ref, i))
        at = pl.multiple_of(i * CH, CH)
        if keep is not None:
            keep[0][pl.ds(at, CH), :] = inv
            keep[1][pl.ds(at, CH), :] = normed
        hid_t[:, pl.ds(at, CH)] = (normed * g_ref[...]).T.astype(BF)
        return carry

    lax.fori_loop(0, TOK // CH, step, 0)


def project(w_ref, off, hid_t, qkv_t):
    for part in range(3):
        p = dot(w_ref[:, part * D + off : part * D + off + HALF], hid_t[...], 0, 0).astype(BF)
        if part == 0:
            p = p * BF(HD**-0.5)
        qkv_t[part * HALF : (part + 1) * HALF, :] = p


def prepare_cotangent(c_ref, wo_ref, off, cot, ga_t):
    def step(i, carry):
        at = pl.multiple_of(i * CH, CH)
        cot[pl.ds(at, CH), :] = rows8(c_ref, i).astype(BF)
        return carry

    lax.fori_loop(0, TOK // CH, step, 0)
    ga_t[...] = dot(wo_ref[off : off + HALF, :], cot[...], 1, 1).astype(BF)


def forward(is_col, qkv_t, att_t, probs):
    qb = TOK // 2

    def head(h, carry):
        at = pl.multiple_of(h * HD, HD)
        sl = pl.ds(at, HD)
        for b in range(2):
            kl = qb * (b + 1)
            qs = slice(b * qb, (b + 1) * qb)
            q = qkv_t[sl, qs]
            k = qkv_t[pl.ds(HALF + at, HD), :kl]
            v = qkv_t[pl.ds(2 * HALF + at, HD), :kl]
            s = dot(k, q, 0, 0)
            gap = (
                lax.broadcasted_iota(jnp.int32, (kl, qb), 1)
                + b * qb
                - lax.broadcasted_iota(jnp.int32, (kl, qb), 0)
            )
            allowed = gap >= 0
            if is_col:
                allowed = jnp.logical_and(allowed, jnp.bitwise_and(gap, 7) == 0)
            s = jnp.where(allowed, s, -1e30)
            e = jnp.exp(s - jnp.max(s, 0, keepdims=True))
            p = e * (1.0 / jnp.sum(e, 0, keepdims=True))
            probs[h, :kl, qs] = p
            att_t[sl, qs] = dot(v, p.astype(BF), 1, 0).astype(BF)
        return carry

    lax.fori_loop(0, HALF // HD, head, 0)


def backward(first, last, qkv_t, ga_t, att_t, probs, d_t):
    qb = TOK // 2

    def head(h, carry):
        at = pl.multiple_of(h * HD, HD)
        sl = pl.ds(at, HD)
        dk = dv = None
        for b in range(2):
            kl = qb * (b + 1)
            qs = slice(b * qb, (b + 1) * qb)
            q = qkv_t[sl, qs]
            k = qkv_t[pl.ds(HALF + at, HD), :kl]
            v = qkv_t[pl.ds(2 * HALF + at, HD), :kl]
            ga = ga_t[sl, qs]
            p = probs[h, :kl, qs]
            delta = jnp.sum(ga.astype(F32) * att_t[sl, qs].astype(F32), 0, keepdims=True)
            ds = (p * (dot(v, ga, 0, 0) - delta)).astype(BF)
            d_t[sl, qs] = (dot(k, ds, 1, 0) * (HD**-0.5)).astype(BF)
            dkb, dvb = dot(q, ds, 1, 1), dot(ga, p.astype(BF), 1, 1)
            if b == 0:
                dk, dv = dkb, dvb
            else:
                dk = jnp.concatenate([dk + dkb[:, :qb], dkb[:, qb:]], 1)
                dv = jnp.concatenate([dv + dvb[:, :qb], dvb[:, qb:]], 1)
        d_t[pl.ds(HALF + at, HD), :] = dk.astype(BF)
        d_t[pl.ds(2 * HALF + at, HD), :] = dv.astype(BF)
        return carry

    lax.fori_loop(first, last, head, 0)


def hidden_grad(w_ref, off, d_t, dh):
    for part in range(3):
        d = d_t[part * HALF : (part + 1) * HALF, :]
        term = dot(d, w_ref[:, part * D + off : part * D + off + HALF], 0, 1)
        if part == 0:
            dh[...] = term
        else:
            dh[...] += term


def qkv_terms(hid_t, d_t, terms):
    for part in range(3):
        d = d_t[part * HALF : (part + 1) * HALF, :]
        at = part * HALF
        terms[:, :, :, at : at + HALF] = dot(hid_t[...], d, 1, 1).reshape(RANKS // 2, 2, 8, HALF)


def out_terms(off, cot, att_t, terms):
    half = slice(off // 16, (off + HALF) // 16)
    terms[half] = dot(att_t[...], cot[...], 1, 0).reshape(HALF // 16, 2, 8, D)


def gain_term(x_ref, dh):
    def step(i, total):
        _, normed = norm_of(rows8(x_ref, i))
        at = pl.multiple_of(i * CH, CH)
        return total + jnp.sum(dh[pl.ds(at, CH), :] * normed, 0, keepdims=True)

    return lax.fori_loop(0, TOK // CH, step, jnp.zeros((1, D), F32))


def kernel(
    x_hbm, c_hbm, g_hbm, w_hbm, wo_hbm,
    out_hbm, gq_ref, go_ref, gg_ref,
    out_ref, x_ref, c_ref, g_ref, w_ref, wo_ref,
    xr, cr, hid_t, cot, qkv_t, ga_t, att_t, d_t, probs, dh_row, dh_col, dh_send, dh_recv,
    terms_a, core_send_a, core_recv_a, plane_send_a, plane_recv_a, z_sum_a, z_send_a, z_recv_a,
    terms_b, core_send_b, core_recv_b, plane_send_b, plane_recv_b, z_sum_b, z_send_b, z_recv_b,
    terms_c, core_send_c, core_recv_c, plane_send_c, plane_recv_c, z_sum_c, z_send_c, z_recv_c,
    inv_row, normed_row, gain_core, gain_pair, gain_plane, gain_planes, gain_z, gain_zs,
    send_sem, recv_sem, own_sem,
):
    me = lax.axis_index("seq")
    line = lax.axis_index("dp")
    core = me % 2
    z_hi = (me // 8) % 2
    my_z = z_hi * LINE + line
    plane = (me // 16) * 4 + (me // 2) % 4
    early = (terms_a, core_send_a, core_recv_a, plane_send_a, plane_recv_a, z_sum_a, z_send_a, z_recv_a)
    middle = (terms_b, core_send_b, core_recv_b, plane_send_b, plane_recv_b, z_sum_b, z_send_b, z_recv_b)
    late = (terms_c, core_send_c, core_recv_c, plane_send_c, plane_recv_c, z_sum_c, z_send_c, z_recv_c)

    def rank_of(other, hi):
        return (other // 4) * 16 + hi * 8 + (other % 4) * 2 + core

    def remote(src, dst, i, target):
        return pltpu.make_async_remote_copy(
            src, dst, send_sem.at[i], recv_sem.at[i], device_id=target, device_id_type=MESH
        )

    def each_peer(f):
        def step(i, carry):
            for t in range(7):
                f(lax.rem(me + 1 + i * 7 + t, RANKS))
            return carry

        lax.fori_loop(0, (RANKS - 1) // 7, step, 0)

    loads = [
        pltpu.make_async_copy(src, dst, own_sem.at[i])
        for i, (src, dst) in enumerate(
            ((x_hbm, x_ref), (g_hbm, g_ref), (w_hbm, w_ref), (c_hbm, c_ref), (wo_hbm, wo_ref))
        )
    ]
    barrier = pltpu.get_barrier_semaphore()
    each_peer(lambda t: pl.semaphore_signal(barrier, inc=1, device_id={"seq": t}, device_id_type=MESH))
    for hi in range(2):
        for t in range(1, LINE):
            pl.semaphore_signal(
                barrier,
                inc=1,
                device_id={"seq": rank_of(plane, hi), "dp": lax.rem(line + t, LINE)},
                device_id_type=MESH,
            )
    for load in loads:
        load.start()
    pl.semaphore_wait(barrier, RANKS - 1 + 2 * (LINE - 1))

    each_peer(lambda t: remote(x_hbm.at[t], xr.at[me], 0, {"seq": t}).start())
    each_peer(lambda t: remote(c_hbm.at[t], cr.at[me], 1, {"seq": t}).start())
    for load in loads:
        load.wait()
    own_x = pltpu.make_async_copy(x_ref.at[me], xr.at[me], own_sem.at[0])
    own_c = pltpu.make_async_copy(c_ref.at[me], cr.at[me], own_sem.at[1])
    own_x.start()
    own_c.start()
    rest = pl.ds(0, RANKS - 1)
    in_x = remote(x_hbm.at[rest], xr.at[rest], 0, {"seq": me})
    in_c = remote(c_hbm.at[rest], cr.at[rest], 1, {"seq": me})

    def core_phase(bufs, i):
        terms, core_send, core_recv = bufs[:3]
        core_send[...] = terms[:, 1 - core].astype(BF)
        pair = remote(core_send, core_recv, i, {"seq": me + 1 - 2 * core})
        pair.start()
        return pair

    def plane_phase(bufs, i, pair):
        terms, _, core_recv, plane_send, plane_recv = bufs[:5]
        pair.wait_recv()
        plane_send[...] = (terms[:, core] + core_recv[...].astype(F32)).astype(BF).reshape(plane_send.shape)
        for t in range(1, 16):
            other = lax.rem(plane + t, 16)
            remote(
                plane_send.at[other // 4, :, other % 4],
                plane_recv.at[plane],
                i,
                {"seq": rank_of(other, z_hi)},
            ).start()
        others = plane_recv.at[pl.ds(0, 15)]
        return remote(others, others, i, {"seq": me})

    def z_phase(bufs, i, plane_in):
        terms, _, core_recv, _, plane_recv, z_sum, z_send, z_recv = bufs
        plane_in.wait_recv()
        for hi in range(2):
            own = rank_of(plane, hi) // 2
            total = terms[own, core] + core_recv[own].astype(F32)
            for t in range(1, 16):
                total += plane_recv[lax.rem(plane + t, 16), hi].astype(F32)
            z_sum[hi] = total
            z_send[hi] = total.astype(BF)
        for t in range(1, 2 * LINE):
            z = lax.rem(my_z + t, 2 * LINE)
            hi = z // LINE
            remote(z_send.at[hi], z_recv.at[my_z], i, {"seq": rank_of(plane, hi), "dp": z % LINE}).start()
        others = z_recv.at[pl.ds(0, 2 * LINE - 1)]
        return remote(others, others, i, {"seq": me})

    def z_total(bufs, z_in):
        z_sum, _, z_recv = bufs[5:]
        z_in.wait_recv()
        total = z_sum[z_hi]
        for t in range(1, 2 * LINE):
            total += z_recv[lax.rem(my_z + t, 2 * LINE)].astype(F32)
        return total

    def gain_plane_phase(pair):
        pair.wait_recv()
        gain_plane[...] = gain_core[...] + gain_pair[...]
        for t in range(1, 16):
            to = rank_of(lax.rem(plane + t, 16), z_hi)
            remote(gain_plane, gain_planes.at[plane], 12, {"seq": to}).start()
        others = gain_planes.at[pl.ds(0, 15)]
        return remote(others, others, 12, {"seq": me})

    def gain_z_phase(plane_in):
        plane_in.wait_recv()
        total = gain_plane[...]
        for t in range(1, 16):
            total += gain_planes[lax.rem(plane + t, 16)]
        gain_z[...] = total
        for t in range(1, 2 * LINE):
            z = lax.rem(my_z + t, 2 * LINE)
            to = {"seq": rank_of(plane, z // LINE), "dp": z % LINE}
            remote(gain_z, gain_zs.at[my_z], 13, to).start()
        others = gain_zs.at[pl.ds(0, 2 * LINE - 1)]
        return remote(others, others, 13, {"seq": me})

    prepare_hidden(x_ref, g_ref, hid_t, (inv_row, normed_row))
    project(w_ref, 0, hid_t, qkv_t)
    forward(False, qkv_t, att_t, probs)
    prepare_cotangent(c_ref, wo_ref, 0, cot, ga_t)
    backward(0, 4, qkv_t, ga_t, att_t, probs, d_t)
    qkv_terms(hid_t, d_t, terms_a)
    pair_a = core_phase(early, 3)
    hidden_grad(w_ref, 0, d_t, dh_row)
    out_terms(0, cot, att_t, terms_b)
    gain_row = gain_term(x_ref, dh_row)
    plane_a = plane_phase(early, 4, pair_a)

    own_x.wait()
    in_x.wait_recv()
    prepare_hidden(xr, g_ref, hid_t)
    project(w_ref, HALF, hid_t, qkv_t)
    forward(True, qkv_t, att_t, probs)
    own_c.wait()
    in_c.wait_recv()
    prepare_cotangent(cr, wo_ref, HALF, cot, ga_t)
    out_terms(HALF, cot, att_t, terms_b)
    pair_b = core_phase(middle, 6)
    z_a = z_phase(early, 5, plane_a)
    backward(0, 2, qkv_t, ga_t, att_t, probs, d_t)
    plane_b = plane_phase(middle, 7, pair_b)
    backward(2, 4, qkv_t, ga_t, att_t, probs, d_t)
    hidden_grad(w_ref, HALF, d_t, dh_col)

    def round_out(i, carry):
        at = pl.multiple_of(i * CH, CH)
        dh_send[pl.ds(i * (CH // 8), CH // 8)] = dh_col[pl.ds(at, CH), :].reshape(CH // 8, 8, D).astype(BF)
        return carry

    lax.fori_loop(0, TOK // CH, round_out, 0)
    each_peer(lambda t: remote(dh_send.at[t], dh_recv.at[me], 2, {"seq": t}).start())
    own_h = pltpu.make_async_copy(dh_send.at[me], dh_recv.at[me], own_sem.at[0])
    own_h.start()
    out_in = remote(dh_send.at[rest], dh_recv.at[rest], 2, {"seq": me})

    qkv_terms(hid_t, d_t, terms_c)
    pair_c = core_phase(late, 9)
    gain = gain_row + gain_term(xr, dh_col)
    gain_core[...] = jnp.zeros((8, 128), F32)
    for i in range(D // 128):
        gain_core[i : i + 1, :] = gain[:, i * 128 : (i + 1) * 128]
    pair_g = remote(gain_core, gain_pair, 14, {"seq": me + 1 - 2 * core})
    pair_g.start()
    plane_c = plane_phase(late, 10, pair_c)
    z_b = z_phase(middle, 8, plane_b)
    plane_g = gain_plane_phase(pair_g)
    z_c = z_phase(late, 11, plane_c)
    z_g = gain_z_phase(plane_g)

    total_a = z_total(early, z_a)
    for part in range(3):
        gq_ref[:, part * D : part * D + HALF] = total_a[:, part * HALF : (part + 1) * HALF]
    go_ref[...] = z_total(middle, z_b)

    own_h.wait()
    out_in.wait_recv()

    def finish(i, carry):
        at = pl.multiple_of(i * CH, CH)
        inv, normed = inv_row[pl.ds(at, CH), :], normed_row[pl.ds(at, CH), :]
        grad_normed = (dh_row[pl.ds(at, CH), :] + rows8(dh_recv, i)) * g_ref[...]
        mean = jnp.mean(grad_normed * normed, -1, keepdims=True)
        grad = rows8(c_ref, i) + inv * (grad_normed - normed * mean)
        part = pl.ds(i * (CH // 8), CH // 8)
        out_ref[part] = grad.astype(BF).reshape(CH // 8, 8, D)
        pltpu.make_async_copy(out_ref.at[part], out_hbm.at[part], own_sem.at[1]).start()
        return carry

    lax.fori_loop(0, TOK // CH, finish, 0)
    out_copy = pltpu.make_async_copy(out_ref, out_hbm, own_sem.at[1])

    total_c = z_total(late, z_c)
    for part in range(3):
        gq_ref[:, part * D + HALF : (part + 1) * D] = total_c[:, part * HALF : (part + 1) * HALF]
    z_g.wait_recv()

    total_g = gain_z[...]
    for t in range(1, 2 * LINE):
        total_g += gain_zs[lax.rem(my_z + t, 2 * LINE)]
    rows = lax.broadcasted_iota(jnp.int32, (8, 128), 0)
    lanes = lax.broadcasted_iota(jnp.int32, (8, 128), 1)
    mine = jnp.sum(jnp.where(rows == me // 16, total_g, 0.0), 0, keepdims=True)
    picked = jnp.where(lanes == (me % 16) * 8 + rows, mine, 0.0)
    gg_ref[...] = jnp.broadcast_to(jnp.sum(picked, 1, keepdims=True), (8, 128))

    out_copy.wait()
    sums = (pair_a, plane_a, z_a, pair_b, plane_b, z_b, pair_c, plane_c, z_c, pair_g, plane_g, z_g)
    for copy in (in_x, in_c, out_in, *sums):
        copy.wait_send()


def deliver(grad, gq, go, gg, grad_out, gq_out, go_out, gg_out, grad_v, gq_v, go_v, gg_v, gain, sem):
    step = RANKS // PIECES
    moves = [(gg, gg_v, gg_out), (gq, gq_v, gq_out), (go, go_v, go_out)]
    moves += [
        tuple(r.at[pl.ds(i * step, step)] for r in (grad, grad_v, grad_out)) for i in range(PIECES)
    ]
    loads = [pltpu.make_async_copy(a, b, sem.at[0, i]) for i, (a, b, _) in enumerate(moves)]
    for load in loads:
        load.start()
    stores = []
    for i, (_, b, c) in enumerate(moves):
        loads[i].wait()
        if i == 0:
            rows = lax.broadcasted_iota(jnp.int32, (8, 128), 0)
            lanes = lax.broadcasted_iota(jnp.int32, (8, 128), 1)
            gain[...] = jnp.sum(jnp.where(rows == lanes, gg_v[...], 0.0), 0, keepdims=True)[:, :8]
            b = gain
        stores.append(pltpu.make_async_copy(b, c, sem.at[1, i]))
        stores[-1].start()
    for store in stores:
        store.wait()


def sum_buffers(cols):
    return [
        pltpu.VMEM((RANKS // 2, 2, 8, cols), F32),
        pltpu.VMEM((RANKS // 2, 8, cols), BF),
        pltpu.VMEM((RANKS // 2, 8, cols), BF),
        pltpu.VMEM((4, 2, 4, 8, cols), BF),
        pltpu.VMEM((16, 2, 8, cols), BF),
        pltpu.VMEM((2, 8, cols), F32),
        pltpu.VMEM((2, 8, cols), BF),
        pltpu.VMEM((2 * LINE, 8, cols), BF),
    ]


def body(inputs, norm_gain, qkv_weight, out_weight, out_cotan):
    vmem = pl.BlockSpec(memory_space=pltpu.VMEM)
    hbm = pl.BlockSpec(memory_space=pl.ANY)
    shapes = (
        jax.ShapeDtypeStruct((RANKS, 8, D), BF),
        jax.ShapeDtypeStruct((8, 3 * D), F32),
        jax.ShapeDtypeStruct((8, D), F32),
    )
    results = pl.pallas_call(
        kernel,
        out_shape=shapes + (jax.ShapeDtypeStruct((8, 128), F32),),
        in_specs=[hbm] * 5,
        out_specs=(hbm, vmem, vmem, vmem),
        scratch_shapes=[
            pltpu.VMEM((RANKS, 8, D), BF),
            pltpu.VMEM((RANKS, 8, D), BF),
            pltpu.VMEM((RANKS, 8, D), BF),
            pltpu.VMEM((1, D), F32),
            pltpu.VMEM((D, 3 * D), BF),
            pltpu.VMEM((D, D), BF),
            pltpu.VMEM((RANKS, 8, D), BF),
            pltpu.VMEM((RANKS, 8, D), BF),
            pltpu.VMEM((D, TOK), BF),
            pltpu.VMEM((TOK, D), BF),
            pltpu.VMEM((3 * HALF, TOK), BF),
            pltpu.VMEM((HALF, TOK), BF),
            pltpu.VMEM((HALF, TOK), BF),
            pltpu.VMEM((3 * HALF, TOK), BF),
            pltpu.VMEM((HALF // HD, TOK, TOK), F32),
            pltpu.VMEM((TOK, D), F32),
            pltpu.VMEM((TOK, D), F32),
            pltpu.VMEM((RANKS, 8, D), BF),
            pltpu.VMEM((RANKS, 8, D), BF),
            *sum_buffers(3 * HALF),
            *sum_buffers(D),
            *sum_buffers(3 * HALF),
            pltpu.VMEM((TOK, 1), F32),
            pltpu.VMEM((TOK, D), F32),
            pltpu.VMEM((8, 128), F32),
            pltpu.VMEM((8, 128), F32),
            pltpu.VMEM((8, 128), F32),
            pltpu.VMEM((16, 8, 128), F32),
            pltpu.VMEM((8, 128), F32),
            pltpu.VMEM((2 * LINE, 8, 128), F32),
            pltpu.SemaphoreType.DMA((15,)),
            pltpu.SemaphoreType.DMA((15,)),
            pltpu.SemaphoreType.DMA((5,)),
        ],
        compiler_params=pltpu.CompilerParams(
            collective_id=0, has_side_effects=True, vmem_limit_bytes=60 * 1024 * 1024
        ),
    )(
        inputs.reshape(RANKS, 8, D),
        out_cotan.reshape(RANKS, 8, D),
        norm_gain.reshape(1, D),
        qkv_weight,
        out_weight,
    )
    grad, grad_qkv, grad_out, grad_gain = pl.pallas_call(
        deliver,
        out_shape=shapes + (jax.ShapeDtypeStruct((1, 8), F32),),
        in_specs=[hbm] * 4,
        out_specs=(hbm,) * 4,
        scratch_shapes=[
            pltpu.VMEM((RANKS, 8, D), BF),
            pltpu.VMEM((8, 3 * D), F32),
            pltpu.VMEM((8, D), F32),
            pltpu.VMEM((8, 128), F32),
            pltpu.VMEM((1, 8), F32),
            pltpu.SemaphoreType.DMA((2, 3 + PIECES)),
        ],
    )(*results)
    return (grad.reshape(inputs.shape), grad_qkv, grad_out, grad_gain.reshape(8))


def solution(mesh):
    return jax.shard_map(
        body,
        mesh=mesh,
        in_specs=(P("dp", "seq", None, None), P(), P(), P(), P("dp", "seq", None, None)),
        out_specs=(P("dp", "seq", None, None), P("seq", None), P("seq", None), P("seq")),
        check_vma=False,
    )
```

```python
import jax
import jax.numpy as jnp
from jax import lax
from jax.experimental import pallas as pl
from jax.experimental.pallas import tpu as pltpu
from jax.sharding import PartitionSpec as P

MESH = pl.DeviceIdType.MESH
BF = jnp.bfloat16
F32 = jnp.float32
TOK = 512
D = 512
HALF = 256
HD = 64
RANKS = 64
LINE = 4
PIECES = 4
CH = 128


def dot(a, b, ca, cb):
    return lax.dot_general(a, b, (((ca,), (cb,)), ((), ())), preferred_element_type=F32)


def rows8(ref, i):
    return ref[pl.ds(i * (CH // 8), CH // 8)].astype(F32).reshape(CH, D)


def norm_of(x):
    inv = lax.rsqrt(jnp.mean(x * x, -1, keepdims=True) + 1e-05)
    return inv, x * inv


def prepare_hidden(x_ref, g_ref, hid_t, keep=None):
    def step(i, carry):
        inv, normed = norm_of(rows8(x_ref, i))
        at = pl.multiple_of(i * CH, CH)
        if keep is not None:
            keep[0][pl.ds(at, CH), :] = inv
            keep[1][pl.ds(at, CH), :] = normed
        hid_t[:, pl.ds(at, CH)] = (normed * g_ref[...]).T.astype(BF)
        return carry

    lax.fori_loop(0, TOK // CH, step, 0)


def project(w_ref, off, hid_t, qkv_t):
    for part in range(3):
        p = dot(w_ref[:, part * D + off : part * D + off + HALF], hid_t[...], 0, 0).astype(BF)
        if part == 0:
            p = p * BF(HD**-0.5)
        qkv_t[part * HALF : (part + 1) * HALF, :] = p


def prepare_cotangent(c_ref, wo_ref, off, cot, ga_t):
    def step(i, carry):
        at = pl.multiple_of(i * CH, CH)
        cot[pl.ds(at, CH), :] = rows8(c_ref, i).astype(BF)
        return carry

    lax.fori_loop(0, TOK // CH, step, 0)
    ga_t[...] = dot(wo_ref[off : off + HALF, :], cot[...], 1, 1).astype(BF)


def forward(is_col, qkv_t, att_t, probs):
    qb = TOK // 2

    def head(h, carry):
        at = pl.multiple_of(h * HD, HD)
        sl = pl.ds(at, HD)
        for b in range(2):
            kl = qb * (b + 1)
            qs = slice(b * qb, (b + 1) * qb)
            q = qkv_t[sl, qs]
            k = qkv_t[pl.ds(HALF + at, HD), :kl]
            v = qkv_t[pl.ds(2 * HALF + at, HD), :kl]
            s = dot(k, q, 0, 0)
            gap = (
                lax.broadcasted_iota(jnp.int32, (kl, qb), 1)
                + b * qb
                - lax.broadcasted_iota(jnp.int32, (kl, qb), 0)
            )
            allowed = gap >= 0
            if is_col:
                allowed = jnp.logical_and(allowed, jnp.bitwise_and(gap, 7) == 0)
            s = jnp.where(allowed, s, -1e30)
            e = jnp.exp(s - jnp.max(s, 0, keepdims=True))
            p = e * (1.0 / jnp.sum(e, 0, keepdims=True))
            probs[h, :kl, qs] = p
            att_t[sl, qs] = dot(v, p.astype(BF), 1, 0).astype(BF)
        return carry

    lax.fori_loop(0, HALF // HD, head, 0)


def backward(first, last, qkv_t, ga_t, att_t, probs, d_t):
    qb = TOK // 2

    def head(h, carry):
        at = pl.multiple_of(h * HD, HD)
        sl = pl.ds(at, HD)
        dk = dv = None
        for b in range(2):
            kl = qb * (b + 1)
            qs = slice(b * qb, (b + 1) * qb)
            q = qkv_t[sl, qs]
            k = qkv_t[pl.ds(HALF + at, HD), :kl]
            v = qkv_t[pl.ds(2 * HALF + at, HD), :kl]
            ga = ga_t[sl, qs]
            p = probs[h, :kl, qs]
            delta = jnp.sum(ga.astype(F32) * att_t[sl, qs].astype(F32), 0, keepdims=True)
            ds = (p * (dot(v, ga, 0, 0) - delta)).astype(BF)
            d_t[sl, qs] = (dot(k, ds, 1, 0) * (HD**-0.5)).astype(BF)
            dkb, dvb = dot(q, ds, 1, 1), dot(ga, p.astype(BF), 1, 1)
            if b == 0:
                dk, dv = dkb, dvb
            else:
                dk = jnp.concatenate([dk + dkb[:, :qb], dkb[:, qb:]], 1)
                dv = jnp.concatenate([dv + dvb[:, :qb], dvb[:, qb:]], 1)
        d_t[pl.ds(HALF + at, HD), :] = dk.astype(BF)
        d_t[pl.ds(2 * HALF + at, HD), :] = dv.astype(BF)
        return carry

    lax.fori_loop(first, last, head, 0)


def hidden_grad(w_ref, off, d_t, dh):
    for part in range(3):
        d = d_t[part * HALF : (part + 1) * HALF, :]
        term = dot(d, w_ref[:, part * D + off : part * D + off + HALF], 0, 1)
        if part == 0:
            dh[...] = term
        else:
            dh[...] += term


def qkv_terms(hid_t, d_t, terms):
    for part in range(3):
        d = d_t[part * HALF : (part + 1) * HALF, :]
        at = part * HALF
        terms[:, :, :, at : at + HALF] = dot(hid_t[...], d, 1, 1).reshape(RANKS // 2, 2, 8, HALF)


def out_terms(off, cot, att_t, terms):
    half = slice(off // 16, (off + HALF) // 16)
    terms[half] = dot(att_t[...], cot[...], 1, 0).reshape(HALF // 16, 2, 8, D)


def gain_term(x_ref, dh):
    def step(i, total):
        _, normed = norm_of(rows8(x_ref, i))
        at = pl.multiple_of(i * CH, CH)
        return total + jnp.sum(dh[pl.ds(at, CH), :] * normed, 0, keepdims=True)

    return lax.fori_loop(0, TOK // CH, step, jnp.zeros((1, D), F32))


def kernel(
    x_hbm, c_hbm, g_hbm, w_hbm, wo_hbm,
    out_hbm, gq_ref, go_ref, gg_ref,
    out_ref, x_ref, c_ref, g_ref, w_ref, wo_ref,
    xr, cr, hid_t, cot, qkv_t, ga_t, att_t, d_t, probs, dh_row, dh_col, dh_send, dh_recv,
    terms_a, core_send_a, core_recv_a, plane_send_a, plane_recv_a, z_sum_a, z_send_a, z_recv_a,
    terms_b, core_send_b, core_recv_b, plane_send_b, plane_recv_b, z_sum_b, z_send_b, z_recv_b,
    terms_c, core_send_c, core_recv_c, plane_send_c, plane_recv_c, z_sum_c, z_send_c, z_recv_c,
    inv_row, normed_row, gain_core, gain_pair, gain_plane, gain_planes, gain_z, gain_zs,
    send_sem, recv_sem, own_sem,
):
    me = lax.axis_index("seq")
    line = lax.axis_index("dp")
    core = me % 2
    z_hi = (me // 8) % 2
    my_z = z_hi * LINE + line
    plane = (me // 16) * 4 + (me // 2) % 4
    early = (terms_a, core_send_a, core_recv_a, plane_send_a, plane_recv_a, z_sum_a, z_send_a, z_recv_a)
    middle = (terms_b, core_send_b, core_recv_b, plane_send_b, plane_recv_b, z_sum_b, z_send_b, z_recv_b)
    late = (terms_c, core_send_c, core_recv_c, plane_send_c, plane_recv_c, z_sum_c, z_send_c, z_recv_c)

    def rank_of(other, hi):
        return (other // 4) * 16 + hi * 8 + (other % 4) * 2 + core

    def remote(src, dst, i, target):
        return pltpu.make_async_remote_copy(
            src, dst, send_sem.at[i], recv_sem.at[i], device_id=target, device_id_type=MESH
        )

    def each_peer(f):
        def step(i, carry):
            for t in range(7):
                f(lax.rem(me + 1 + i * 7 + t, RANKS))
            return carry

        lax.fori_loop(0, (RANKS - 1) // 7, step, 0)

    loads = [
        pltpu.make_async_copy(src, dst, own_sem.at[i])
        for i, (src, dst) in enumerate(
            ((x_hbm, x_ref), (g_hbm, g_ref), (w_hbm, w_ref), (c_hbm, c_ref), (wo_hbm, wo_ref))
        )
    ]
    barrier = pltpu.get_barrier_semaphore()
    each_peer(lambda t: pl.semaphore_signal(barrier, inc=1, device_id={"seq": t}, device_id_type=MESH))
    for hi in range(2):
        for t in range(1, LINE):
            pl.semaphore_signal(
                barrier,
                inc=1,
                device_id={"seq": rank_of(plane, hi), "dp": lax.rem(line + t, LINE)},
                device_id_type=MESH,
            )
    for load in loads:
        load.start()
    pl.semaphore_wait(barrier, RANKS - 1 + 2 * (LINE - 1))

    each_peer(lambda t: remote(x_hbm.at[t], xr.at[me], 0, {"seq": t}).start())
    each_peer(lambda t: remote(c_hbm.at[t], cr.at[me], 1, {"seq": t}).start())
    for load in loads:
        load.wait()
    own_x = pltpu.make_async_copy(x_ref.at[me], xr.at[me], own_sem.at[0])
    own_c = pltpu.make_async_copy(c_ref.at[me], cr.at[me], own_sem.at[1])
    own_x.start()
    own_c.start()
    rest = pl.ds(0, RANKS - 1)
    in_x = remote(x_hbm.at[rest], xr.at[rest], 0, {"seq": me})
    in_c = remote(c_hbm.at[rest], cr.at[rest], 1, {"seq": me})

    def core_phase(bufs, i):
        terms, core_send, core_recv = bufs[:3]
        core_send[...] = terms[:, 1 - core].astype(BF)
        pair = remote(core_send, core_recv, i, {"seq": me + 1 - 2 * core})
        pair.start()
        return pair

    def plane_phase(bufs, i, pair):
        terms, _, core_recv, plane_send, plane_recv = bufs[:5]
        pair.wait_recv()
        plane_send[...] = (terms[:, core] + core_recv[...].astype(F32)).astype(BF).reshape(plane_send.shape)
        for t in range(1, 16):
            other = lax.rem(plane + t, 16)
            remote(
                plane_send.at[other // 4, :, other % 4],
                plane_recv.at[plane],
                i,
                {"seq": rank_of(other, z_hi)},
            ).start()
        others = plane_recv.at[pl.ds(0, 15)]
        return remote(others, others, i, {"seq": me})

    def z_phase(bufs, i, plane_in):
        terms, _, core_recv, _, plane_recv, z_sum, z_send, z_recv = bufs
        plane_in.wait_recv()
        for hi in range(2):
            own = rank_of(plane, hi) // 2
            total = terms[own, core] + core_recv[own].astype(F32)
            for t in range(1, 16):
                total += plane_recv[lax.rem(plane + t, 16), hi].astype(F32)
            z_sum[hi] = total
            z_send[hi] = total.astype(BF)
        for t in range(1, 2 * LINE):
            z = lax.rem(my_z + t, 2 * LINE)
            hi = z // LINE
            remote(z_send.at[hi], z_recv.at[my_z], i, {"seq": rank_of(plane, hi), "dp": z % LINE}).start()
        others = z_recv.at[pl.ds(0, 2 * LINE - 1)]
        return remote(others, others, i, {"seq": me})

    def z_total(bufs, z_in):
        z_sum, _, z_recv = bufs[5:]
        z_in.wait_recv()
        total = z_sum[z_hi]
        for t in range(1, 2 * LINE):
            total += z_recv[lax.rem(my_z + t, 2 * LINE)].astype(F32)
        return total

    def gain_plane_phase(pair):
        pair.wait_recv()
        gain_plane[...] = gain_core[...] + gain_pair[...]
        for t in range(1, 16):
            to = rank_of(lax.rem(plane + t, 16), z_hi)
            remote(gain_plane, gain_planes.at[plane], 12, {"seq": to}).start()
        others = gain_planes.at[pl.ds(0, 15)]
        return remote(others, others, 12, {"seq": me})

    def gain_z_phase(plane_in):
        plane_in.wait_recv()
        total = gain_plane[...]
        for t in range(1, 16):
            total += gain_planes[lax.rem(plane + t, 16)]
        gain_z[...] = total
        for t in range(1, 2 * LINE):
            z = lax.rem(my_z + t, 2 * LINE)
            to = {"seq": rank_of(plane, z // LINE), "dp": z % LINE}
            remote(gain_z, gain_zs.at[my_z], 13, to).start()
        others = gain_zs.at[pl.ds(0, 2 * LINE - 1)]
        return remote(others, others, 13, {"seq": me})

    prepare_hidden(x_ref, g_ref, hid_t, (inv_row, normed_row))
    project(w_ref, 0, hid_t, qkv_t)
    forward(False, qkv_t, att_t, probs)
    prepare_cotangent(c_ref, wo_ref, 0, cot, ga_t)
    backward(0, 4, qkv_t, ga_t, att_t, probs, d_t)
    qkv_terms(hid_t, d_t, terms_a)
    pair_a = core_phase(early, 3)
    hidden_grad(w_ref, 0, d_t, dh_row)
    out_terms(0, cot, att_t, terms_b)
    gain_row = gain_term(x_ref, dh_row)
    plane_a = plane_phase(early, 4, pair_a)

    own_x.wait()
    in_x.wait_recv()
    prepare_hidden(xr, g_ref, hid_t)
    project(w_ref, HALF, hid_t, qkv_t)
    forward(True, qkv_t, att_t, probs)
    own_c.wait()
    in_c.wait_recv()
    prepare_cotangent(cr, wo_ref, HALF, cot, ga_t)
    out_terms(HALF, cot, att_t, terms_b)
    pair_b = core_phase(middle, 6)
    z_a = z_phase(early, 5, plane_a)
    backward(0, 1, qkv_t, ga_t, att_t, probs, d_t)
    plane_b = plane_phase(middle, 7, pair_b)
    backward(1, 4, qkv_t, ga_t, att_t, probs, d_t)
    hidden_grad(w_ref, HALF, d_t, dh_col)

    def round_out(i, carry):
        at = pl.multiple_of(i * CH, CH)
        dh_send[pl.ds(i * (CH // 8), CH // 8)] = dh_col[pl.ds(at, CH), :].reshape(CH // 8, 8, D).astype(BF)
        return carry

    lax.fori_loop(0, TOK // CH, round_out, 0)
    each_peer(lambda t: remote(dh_send.at[t], dh_recv.at[me], 2, {"seq": t}).start())
    own_h = pltpu.make_async_copy(dh_send.at[me], dh_recv.at[me], own_sem.at[0])
    own_h.start()
    out_in = remote(dh_send.at[rest], dh_recv.at[rest], 2, {"seq": me})

    qkv_terms(hid_t, d_t, terms_c)
    pair_c = core_phase(late, 9)
    gain = gain_row + gain_term(xr, dh_col)
    gain_core[...] = jnp.zeros((8, 128), F32)
    for i in range(D // 128):
        gain_core[i : i + 1, :] = gain[:, i * 128 : (i + 1) * 128]
    pair_g = remote(gain_core, gain_pair, 14, {"seq": me + 1 - 2 * core})
    pair_g.start()
    plane_c = plane_phase(late, 10, pair_c)
    z_b = z_phase(middle, 8, plane_b)
    plane_g = gain_plane_phase(pair_g)
    z_c = z_phase(late, 11, plane_c)
    z_g = gain_z_phase(plane_g)

    total_a = z_total(early, z_a)
    for part in range(3):
        gq_ref[:, part * D : part * D + HALF] = total_a[:, part * HALF : (part + 1) * HALF]
    go_ref[...] = z_total(middle, z_b)

    own_h.wait()
    out_in.wait_recv()

    def finish(i, carry):
        at = pl.multiple_of(i * CH, CH)
        inv, normed = inv_row[pl.ds(at, CH), :], normed_row[pl.ds(at, CH), :]
        grad_normed = (dh_row[pl.ds(at, CH), :] + rows8(dh_recv, i)) * g_ref[...]
        mean = jnp.mean(grad_normed * normed, -1, keepdims=True)
        grad = rows8(c_ref, i) + inv * (grad_normed - normed * mean)
        part = pl.ds(i * (CH // 8), CH // 8)
        out_ref[part] = grad.astype(BF).reshape(CH // 8, 8, D)
        pltpu.make_async_copy(out_ref.at[part], out_hbm.at[part], own_sem.at[1]).start()
        return carry

    lax.fori_loop(0, TOK // CH, finish, 0)
    out_copy = pltpu.make_async_copy(out_ref, out_hbm, own_sem.at[1])

    total_c = z_total(late, z_c)
    for part in range(3):
        gq_ref[:, part * D + HALF : (part + 1) * D] = total_c[:, part * HALF : (part + 1) * HALF]
    z_g.wait_recv()

    total_g = gain_z[...]
    for t in range(1, 2 * LINE):
        total_g += gain_zs[lax.rem(my_z + t, 2 * LINE)]
    rows = lax.broadcasted_iota(jnp.int32, (8, 128), 0)
    lanes = lax.broadcasted_iota(jnp.int32, (8, 128), 1)
    mine = jnp.sum(jnp.where(rows == me // 16, total_g, 0.0), 0, keepdims=True)
    picked = jnp.where(lanes == (me % 16) * 8 + rows, mine, 0.0)
    gg_ref[...] = jnp.broadcast_to(jnp.sum(picked, 1, keepdims=True), (8, 128))

    out_copy.wait()
    sums = (pair_a, plane_a, z_a, pair_b, plane_b, z_b, pair_c, plane_c, z_c, pair_g, plane_g, z_g)
    for copy in (in_x, in_c, out_in, *sums):
        copy.wait_send()


def deliver(grad, gq, go, gg, grad_out, gq_out, go_out, gg_out, grad_v, gq_v, go_v, gg_v, gain, sem):
    step = RANKS // PIECES
    moves = [(gg, gg_v, gg_out), (gq, gq_v, gq_out), (go, go_v, go_out)]
    moves += [
        tuple(r.at[pl.ds(i * step, step)] for r in (grad, grad_v, grad_out)) for i in range(PIECES)
    ]
    loads = [pltpu.make_async_copy(a, b, sem.at[0, i]) for i, (a, b, _) in enumerate(moves)]
    for load in loads:
        load.start()
    stores = []
    for i, (_, b, c) in enumerate(moves):
        loads[i].wait()
        if i == 0:
            rows = lax.broadcasted_iota(jnp.int32, (8, 128), 0)
            lanes = lax.broadcasted_iota(jnp.int32, (8, 128), 1)
            gain[...] = jnp.sum(jnp.where(rows == lanes, gg_v[...], 0.0), 0, keepdims=True)[:, :8]
            b = gain
        stores.append(pltpu.make_async_copy(b, c, sem.at[1, i]))
        stores[-1].start()
    for store in stores:
        store.wait()


def sum_buffers(cols):
    return [
        pltpu.VMEM((RANKS // 2, 2, 8, cols), F32),
        pltpu.VMEM((RANKS // 2, 8, cols), BF),
        pltpu.VMEM((RANKS // 2, 8, cols), BF),
        pltpu.VMEM((4, 2, 4, 8, cols), BF),
        pltpu.VMEM((16, 2, 8, cols), BF),
        pltpu.VMEM((2, 8, cols), F32),
        pltpu.VMEM((2, 8, cols), BF),
        pltpu.VMEM((2 * LINE, 8, cols), BF),
    ]


def body(inputs, norm_gain, qkv_weight, out_weight, out_cotan):
    vmem = pl.BlockSpec(memory_space=pltpu.VMEM)
    hbm = pl.BlockSpec(memory_space=pl.ANY)
    shapes = (
        jax.ShapeDtypeStruct((RANKS, 8, D), BF),
        jax.ShapeDtypeStruct((8, 3 * D), F32),
        jax.ShapeDtypeStruct((8, D), F32),
    )
    results = pl.pallas_call(
        kernel,
        out_shape=shapes + (jax.ShapeDtypeStruct((8, 128), F32),),
        in_specs=[hbm] * 5,
        out_specs=(hbm, vmem, vmem, vmem),
        scratch_shapes=[
            pltpu.VMEM((RANKS, 8, D), BF),
            pltpu.VMEM((RANKS, 8, D), BF),
            pltpu.VMEM((RANKS, 8, D), BF),
            pltpu.VMEM((1, D), F32),
            pltpu.VMEM((D, 3 * D), BF),
            pltpu.VMEM((D, D), BF),
            pltpu.VMEM((RANKS, 8, D), BF),
            pltpu.VMEM((RANKS, 8, D), BF),
            pltpu.VMEM((D, TOK), BF),
            pltpu.VMEM((TOK, D), BF),
            pltpu.VMEM((3 * HALF, TOK), BF),
            pltpu.VMEM((HALF, TOK), BF),
            pltpu.VMEM((HALF, TOK), BF),
            pltpu.VMEM((3 * HALF, TOK), BF),
            pltpu.VMEM((HALF // HD, TOK, TOK), F32),
            pltpu.VMEM((TOK, D), F32),
            pltpu.VMEM((TOK, D), F32),
            pltpu.VMEM((RANKS, 8, D), BF),
            pltpu.VMEM((RANKS, 8, D), BF),
            *sum_buffers(3 * HALF),
            *sum_buffers(D),
            *sum_buffers(3 * HALF),
            pltpu.VMEM((TOK, 1), F32),
            pltpu.VMEM((TOK, D), F32),
            pltpu.VMEM((8, 128), F32),
            pltpu.VMEM((8, 128), F32),
            pltpu.VMEM((8, 128), F32),
            pltpu.VMEM((16, 8, 128), F32),
            pltpu.VMEM((8, 128), F32),
            pltpu.VMEM((2 * LINE, 8, 128), F32),
            pltpu.SemaphoreType.DMA((15,)),
            pltpu.SemaphoreType.DMA((15,)),
            pltpu.SemaphoreType.DMA((5,)),
        ],
        compiler_params=pltpu.CompilerParams(
            collective_id=0, has_side_effects=True, vmem_limit_bytes=60 * 1024 * 1024
        ),
    )(
        inputs.reshape(RANKS, 8, D),
        out_cotan.reshape(RANKS, 8, D),
        norm_gain.reshape(1, D),
        qkv_weight,
        out_weight,
    )
    grad, grad_qkv, grad_out, grad_gain = pl.pallas_call(
        deliver,
        out_shape=shapes + (jax.ShapeDtypeStruct((1, 8), F32),),
        in_specs=[hbm] * 4,
        out_specs=(hbm,) * 4,
        scratch_shapes=[
            pltpu.VMEM((RANKS, 8, D), BF),
            pltpu.VMEM((8, 3 * D), F32),
            pltpu.VMEM((8, D), F32),
            pltpu.VMEM((8, 128), F32),
            pltpu.VMEM((1, 8), F32),
            pltpu.SemaphoreType.DMA((2, 3 + PIECES)),
        ],
    )(*results)
    return (grad.reshape(inputs.shape), grad_qkv, grad_out, grad_gain.reshape(8))


def solution(mesh):
    return jax.shard_map(
        body,
        mesh=mesh,
        in_specs=(P("dp", "seq", None, None), P(), P(), P(), P("dp", "seq", None, None)),
        out_specs=(P("dp", "seq", None, None), P("seq", None), P("seq", None), P("seq")),
        check_vma=False,
    )
```
